32 devices in a mesh: row: 4 (over x, core), col: 8 (over z, y).
Axes of the slice: x: 2, y: 2, z: 4, core: 2. Of those that a mesh axis runs over, the one named last changes fastest.
Arguments:
- inputs: bfloat16 [512, 12288], P('row', 'col'), may hold values from -6 to 6
- out_grad: bfloat16 [512, 12288], P('row', 'col'), may hold values from -1.5 to 1.5
- first_vals: bfloat16 [4, 8, 512, 128, 128], P('row', 'col'), may hold values from -0.109375 to 0.109375
- first_rows: int32 [4, 8, 512], P('row', 'col'), may hold values from 0 to 11, as said below
- first_cols: int32 [4, 8, 512], P('row', 'col'), may hold values from 0 to 95
- first_count: int32 [4, 8], P('row', 'col'), may hold values from 64 to 512, as said below
- second_vals: bfloat16 [4, 8, 512, 128, 128], P('row', 'col'), may hold values from -0.0546875 to 0.0546875
- second_rows: int32 [4, 8, 512], P('row', 'col'), may hold values from 0 to 95, as said below
- second_cols: int32 [4, 8, 512], P('row', 'col'), may hold values from 0 to 11
- second_count: int32 [4, 8], P('row', 'col'), may hold values from 64 to 512, as said below
Outputs:
- layer_out: bfloat16 [512, 12288], P('row', 'col')
- input_grad: bfloat16 [512, 12288], P('row', 'col')
- first_grad: bfloat16 [4, 8, 512, 128, 128], P('row', 'col')
- second_grad: bfloat16 [4, 8, 512, 128, 128], P('row', 'col')
The draws below stay inside these ranges and needn't reach their ends.
Inputs may be any that keep to these rules, and one draw needn't show every extreme that they name: Within one tile the slots name distinct blocks; slot s of tile (i, j) holds block (first_rows, first_cols) of that tile's 12 x 96 grid. The live slots are slots 0 to first_count - 1; some tile has all 512 slots live in every draw. `second_rows`: within one tile the slots name distinct blocks of that tile's 96 x 12 grid. The live slots are slots 0 to second_count - 1; some tile has all 512 slots live in every draw.
All inputs are finite; a program needn't handle non-finite values.
Results may differ from the reference program's by a relative error of at most 0.018.
Values may be sent and summed in bfloat16 or wider, within the bound.
No kernel may reach another device: no remote copies, remote signals or barrier semaphores. Data moves between devices by JAX's collectives and lax.ppermute only.
A program may use at most 640 MiB of HBM per device.

```python
import jax
import jax.numpy as jnp
from jax import lax

D = 12288
FF = 49152
BLK = 128
TOKENS = 512
DB = 12
FB = 96
CAP = 512
N_ROW = 4
N_COL = 8


def tile_layout(key, marker):
    layout_key = jax.random.fold_in(key, marker)
    perm_key, count_key, full_key, pick_key = jax.random.split(layout_key, 4)
    tiles = N_ROW * N_COL
    tile_keys = jax.random.split(perm_key, tiles)
    positions = jax.vmap(lambda one_key: jax.random.permutation(one_key, DB * FB)[:CAP])(tile_keys)
    counts = jax.random.randint(count_key, (tiles,), CAP // 8, CAP - CAP // 8 + 1)
    filled = jax.random.randint(full_key, (tiles,), 0, 8) == 0
    chosen = jax.random.randint(pick_key, (), 0, tiles)
    filled = filled | (jnp.arange(tiles) == chosen)
    counts = jnp.where(filled, CAP, counts)
    return (positions.reshape(N_ROW, N_COL, CAP).astype(jnp.int32), counts.reshape(N_ROW, N_COL).astype(jnp.int32))


def draw_first_rows(key, part):
    positions, _ = tile_layout(key, 101)
    return (positions // FB).astype(jnp.int32)


def draw_first_cols(key, part):
    positions, _ = tile_layout(key, 101)
    return (positions % FB).astype(jnp.int32)


def draw_first_count(key, part):
    _, counts = tile_layout(key, 101)
    return counts


def draw_second_rows(key, part):
    positions, _ = tile_layout(key, 202)
    return (positions // DB).astype(jnp.int32)


def draw_second_cols(key, part):
    positions, _ = tile_layout(key, 202)
    return (positions % DB).astype(jnp.int32)


def draw_second_count(key, part):
    _, counts = tile_layout(key, 202)
    return counts


def level_of(own_key, shape, pieces, smallest, largest):
    loudness, own = 1.0, jax.random.fold_in(own_key, 6)
    for axis_at, parts in pieces:
        steps = jnp.exp(jax.random.uniform(jax.random.fold_in(own, axis_at), (parts,), jnp.float32, smallest / len(pieces), largest / len(pieces)))
        loudness = loudness * jnp.repeat(steps, shape[axis_at] // parts).reshape([-1 if axis == axis_at else 1 for axis in range(len(shape))])
    return loudness


def bell_draw(key, extent, spread, limit, pieces=(), kind=jnp.bfloat16):
    factor_of = level_of(key, extent, pieces, -0.22, 0.18) if pieces else 1.0
    values = jax.random.normal(key, extent, jnp.float32) * spread * factor_of
    return jnp.minimum(jnp.maximum(values, -limit), limit).astype(kind)


def setup_inputs(seed: int = 0) -> dict:
    splits = jax.random.split(jax.random.key(seed), 11)
    return {
        "inputs": bell_draw(splits[0], (TOKENS, D), 1.0, 6.0, ((0, 4), (1, 8))),
        "out_grad": bell_draw(splits[1], (TOKENS, D), 0.25, 1.5, ((0, 4), (1, 8))),
        "first_vals": bell_draw(splits[2], (N_ROW, N_COL, CAP, BLK, BLK), (D // 4) ** -0.5, 0.109375, ((0, 4), (1, 8))),
        "first_rows": draw_first_rows(jax.random.fold_in(splits[10], 71), 0),
        "first_cols": draw_first_cols(jax.random.fold_in(splits[10], 71), 0),
        "first_count": draw_first_count(jax.random.fold_in(splits[10], 71), 0),
        "second_vals": bell_draw(splits[6], (N_ROW, N_COL, CAP, BLK, BLK), (FF // 4) ** -0.5, 0.0546875, ((0, 4), (1, 8))),
        "second_rows": draw_second_rows(jax.random.fold_in(splits[10], 71), 0),
        "second_cols": draw_second_cols(jax.random.fold_in(splits[10], 71), 0),
        "second_count": draw_second_count(jax.random.fold_in(splits[10], 71), 0),
    }


HIGH = lax.Precision.HIGHEST

def activate(value):
    return jax.nn.gelu(value, approximate=True)

def live_slots(count, slots):
    return (jnp.arange(slots, dtype=jnp.int32) < count).astype(jnp.float32)

def block_apply(blocks_in, first, second, count, vals, n_out, flip):
    picked = jnp.take(blocks_in, first, axis=1).astype(jnp.float32)
    weights = vals.astype(jnp.float32)
    if flip:
        product = jnp.einsum('tsk,snk->tsn', picked, weights, precision=HIGH)
    else:
        product = jnp.einsum('tsk,skn->tsn', picked, weights, precision=HIGH)
    route = (second[:, None] == jnp.arange(n_out, dtype=jnp.int32)[None, :]).astype(jnp.float32)
    route = route * live_slots(count, first.shape[0])[:, None]
    return jnp.einsum('tsn,so->ton', product, route, precision=HIGH)

def grid_sum(stack, vals, first, second, counts, n_out, flip, rounded):

    def step(total, item):
        blocks_in, tile_vals, first_idx, second_idx, count = item
        part = block_apply(blocks_in, first_idx, second_idx, count, tile_vals, n_out, flip)
        if rounded:
            part = lax.optimization_barrier(part.astype(jnp.bfloat16)).astype(jnp.float32)
        return (total + part, None)
    start_total = jnp.zeros((stack.shape[1], n_out, BLK), jnp.float32)
    total, _ = lax.scan(step, start_total, (stack, vals, first, second, counts))
    return total

def tile_grads(left_stack, left_by_row, right_stack, left_idx, right_idx, counts):
    row_ids = jnp.repeat(jnp.arange(N_ROW, dtype=jnp.int32), N_COL)
    col_ids = jnp.tile(jnp.arange(N_COL, dtype=jnp.int32), N_ROW)

    def one_tile(item):
        row_id, col_id, left_sel, right_sel, count = item
        if left_by_row:
            left = left_stack[row_id]
            right = right_stack[col_id]
        else:
            left = left_stack[col_id]
            right = right_stack[row_id]
        left_pick = jnp.take(left, left_sel, axis=1).astype(jnp.float32)
        right_pick = jnp.take(right, right_sel, axis=1).astype(jnp.float32)
        grads = jnp.einsum('tsk,tsn->skn', left_pick, right_pick, precision=HIGH)
        grads = grads * live_slots(count, left_sel.shape[0])[:, None, None]
        return grads.astype(jnp.bfloat16)
    result = lax.map(one_tile, (row_ids, col_ids, left_idx.reshape(N_ROW * N_COL, CAP), right_idx.reshape(N_ROW * N_COL, CAP), counts.reshape(N_ROW * N_COL)))
    return result.reshape(N_ROW, N_COL, CAP, BLK, BLK)

def swapped(array):
    return jnp.swapaxes(array, 0, 1)

def reference(inputs, out_grad, first_vals, first_rows, first_cols, first_count, second_vals, second_rows, second_cols, second_count):
    x_groups = inputs.reshape(TOKENS, N_COL, DB, BLK).transpose(1, 0, 2, 3)
    grad_groups = out_grad.reshape(TOKENS, N_COL, DB, BLK).transpose(1, 0, 2, 3)

    def hidden_row(item):
        return grid_sum(x_groups, item[0], item[1], item[2], item[3], FB, False, True)
    hidden = lax.map(hidden_row, (first_vals, first_rows, first_cols, first_count))
    hidden = hidden.transpose(1, 0, 2, 3).reshape(TOKENS, FF)
    activated = activate(hidden).astype(jnp.bfloat16)
    act_groups = activated.reshape(TOKENS, N_ROW, FB, BLK).transpose(1, 0, 2, 3)

    def out_col(item):
        return grid_sum(act_groups, item[0], item[1], item[2], item[3], DB, False, False)
    layer_out = lax.map(out_col, (swapped(second_vals), swapped(second_rows), swapped(second_cols), swapped(second_count)))
    layer_out = layer_out.transpose(1, 0, 2, 3).reshape(TOKENS, D).astype(jnp.bfloat16)

    def grad_row(item):
        return grid_sum(grad_groups, item[0], item[1], item[2], item[3], FB, True, True)
    act_grad = lax.map(grad_row, (second_vals, second_cols, second_rows, second_count))
    act_grad = act_grad.transpose(1, 0, 2, 3).reshape(TOKENS, FF)
    _, pullback = jax.vjp(activate, hidden)
    hid_grad = pullback(act_grad)[0].astype(jnp.bfloat16)
    hid_groups = hid_grad.reshape(TOKENS, N_ROW, FB, BLK).transpose(1, 0, 2, 3)

    def input_col(item):
        return grid_sum(hid_groups, item[0], item[1], item[2], item[3], DB, True, False)
    input_grad = lax.map(input_col, (swapped(first_vals), swapped(first_cols), swapped(first_rows), swapped(first_count)))
    input_grad = input_grad.transpose(1, 0, 2, 3).reshape(TOKENS, D).astype(jnp.bfloat16)
    first_grad = tile_grads(x_groups, False, hid_groups, first_rows, first_cols, first_count)
    second_grad = tile_grads(act_groups, True, grad_groups, second_rows, second_cols, second_count)
    return (layer_out, input_grad, first_grad, second_grad)
```

```python
import functools

import jax
import jax.numpy as jnp
from jax import lax
from jax.experimental import pallas as pl
from jax.experimental.pallas import tpu as pltpu
from jax.sharding import PartitionSpec as P

BLK = 128
Z_CHIPS = 4
ROOT_2_PI = 0.7978845608028654
CUBIC = 0.044715
VMEM_LIMIT = 40 << 20


def ring_of(n):
    if n % Z_CHIPS or n // Z_CHIPS < 2:
        return list(range(n))
    wide = n // Z_CHIPS
    order = [z * wide for z in range(Z_CHIPS)]
    for k, z in enumerate(reversed(range(Z_CHIPS))):
        ys = range(1, wide) if k % 2 == 0 else range(wide - 1, 0, -1)
        order += [z * wide + y for y in ys]
    return order


def gelu_pair(value, grad):
    inner = ROOT_2_PI * (value + CUBIC * (value * value * value))
    th = jnp.tanh(inner)
    half = 0.5 * (1.0 + th)
    slope = half + 0.5 * value * (1.0 - th * th) * (ROOT_2_PI * (1.0 + (3.0 * CUBIC) * (value * value)))
    return value * half, grad * slope


def block_table(first, second, count, n_second, n_total):
    slots = first.shape[0]
    ids = jnp.arange(slots, dtype=jnp.int32)
    key = jnp.where(ids < count, first * n_second + second, -1)
    hit = key[None, :] == jnp.arange(n_total, dtype=jnp.int32)[:, None]
    return jnp.max(jnp.where(hit, ids[None, :], -1), axis=1)


class Tiles:
    def __init__(self, base, tab1, tab2, vals1, vals2, buf1, buf2, sems, sizes, width):
        self.args = (tab1, tab2, vals1, vals2, buf1, buf2, sems)
        self.width = width
        self.blocks = []
        for g, size in enumerate(sizes):
            for k in range(size):
                self.blocks.append((base[g] + k) * width)

    def place(self, which, b, r):
        tab1, tab2, vals1, vals2, buf1, buf2, sems = self.args
        wide = pl.ds(pl.multiple_of(r * BLK, BLK), BLK)
        if which == 0:
            return tab1, vals1, buf1.at[wide, pl.ds(b * BLK, BLK)], sems.at[0, b, r]
        return tab2, vals2, buf2.at[pl.ds(b * BLK, BLK), wide], sems.at[1, b, r]

    def start(self):
        def step(r, carry):
            for which in (0, 1):
                for b, row in enumerate(self.blocks):
                    tab, vals, dst, sem = self.place(which, b, r)
                    slot = tab[row + r]

                    @pl.when(slot >= 0)
                    def _():
                        pltpu.make_async_copy(vals.at[jnp.maximum(slot, 0)], dst, sem).start()

                    @pl.when(slot < 0)
                    def _():
                        dst[...] = jnp.zeros((BLK, BLK), dst.dtype)
            return carry

        lax.fori_loop(0, self.width, step, 0)

    def wait(self):
        def step(r, carry):
            for which in (0, 1):
                for b, row in enumerate(self.blocks):
                    tab, vals, dst, sem = self.place(which, b, r)

                    @pl.when(tab[row + r] >= 0)
                    def _():
                        pltpu.make_async_copy(vals.at[0], dst, sem).wait()
            return carry

        lax.fori_loop(0, self.width, step, 0)


def dot_nn(a, b):
    return jnp.dot(a, b, preferred_element_type=jnp.float32)


def dot_nt(a, b):
    return lax.dot_general(a, b, (((1,), (1,)), ((), ())), preferred_element_type=jnp.float32)


def dot_tn(a, b):
    return lax.dot_general(a, b, (((0,), (0,)), ((), ())), preferred_element_type=jnp.float32)


def up_kernel(sizes, width, has_in, last, *refs):
    base, tab1, tab2, x, dy, vals1, vals2 = refs[:7]
    refs = refs[7:]
    n = len(sizes)
    ins = refs[:n] if has_in else [None] * n
    refs = refs[n:] if has_in else refs
    outs, refs = refs[:n], refs[n:]
    buf1, buf2, sems = refs
    tiles = Tiles(base, tab1, tab2, vals1, vals2, buf1, buf2, sems, sizes, width)
    tiles.start()
    tiles.wait()
    where = [(g, k) for g, size in enumerate(sizes) for k in range(size)]
    total = len(where)
    for lo in range(0, total, 2):
        cnt = min(2, total - lo)
        span = pl.ds(lo * BLK, cnt * BLK)
        hid = dot_nn(x[...], buf1[:, span])
        grd = dot_nt(dy[...], buf2[span, :])
        for i in range(cnt):
            g, k = where[lo + i]
            at = pl.ds(k * BLK, BLK)
            h = hid[:, i * BLK : (i + 1) * BLK]
            d = grd[:, i * BLK : (i + 1) * BLK]
            if has_in:
                h = h + ins[g][0, :, at].astype(jnp.float32)
                d = d + ins[g][1, :, at].astype(jnp.float32)
            if last:
                h, d = gelu_pair(h, d)
            outs[g][0, :, at] = h.astype(jnp.bfloat16)
            outs[g][1, :, at] = d.astype(jnp.bfloat16)


def smem():
    return pl.BlockSpec(memory_space=pltpu.SMEM)


def vmem():
    return pl.BlockSpec(memory_space=pltpu.VMEM)


def hbm():
    return pl.BlockSpec(memory_space=pl.ANY)


def tile_scratch(total, width):
    return [
        pltpu.VMEM((width * BLK, total * BLK), jnp.bfloat16),
        pltpu.VMEM((total * BLK, width * BLK), jnp.bfloat16),
        pltpu.SemaphoreType.DMA((2, total, width)),
    ]


def up_call(sizes, width, base, tabs, x, dy, vals, ins, last):
    total = sum(sizes)
    tokens = x.shape[0]
    has_in = ins is not None
    return pl.pallas_call(
        functools.partial(up_kernel, sizes, width, has_in, last),
        out_shape=[jax.ShapeDtypeStruct((2, tokens, s * BLK), jnp.bfloat16) for s in sizes],
        in_specs=[smem()] * 3 + [vmem()] * 2 + [hbm()] * 2 + [vmem()] * (len(sizes) if has_in else 0),
        out_specs=[vmem()] * len(sizes),
        scratch_shapes=tile_scratch(total, width),
        compiler_params=pltpu.CompilerParams(vmem_limit_bytes=VMEM_LIMIT),
        cost_estimate=pl.CostEstimate(
            flops=4 * tokens * width * total * BLK * BLK,
            bytes_accessed=4 * width * total * BLK * BLK + 8 * tokens * total * BLK,
            transcendentals=0,
        ),
        name="up_last" if last else "up",
    )(base, *tabs, x, dy, *vals, *(ins if has_in else ()))


def down_kernel(sizes, width, first, last, *refs):
    base, tab1, tab2, vals1, vals2 = refs[:5]
    refs = refs[5:]
    n = len(sizes)
    acts, refs = refs[:n], refs[n:]
    if not first:
        out_in, in_in = refs[:2]
        refs = refs[2:]
    out_o, in_o, buf1, buf2, sems = refs
    step = pl.program_id(0)

    @pl.when(step == 0)
    def _():
        tiles = Tiles(base, tab1, tab2, vals1, vals2, buf1, buf2, sems, sizes, width)
        tiles.start()
        tiles.wait()

    wide = out_o.shape[1]
    span = pl.ds(pl.multiple_of(step * wide, BLK), wide)
    act = jnp.concatenate([a[0] for a in acts], axis=1)
    grd = jnp.concatenate([a[1] for a in acts], axis=1)
    out = dot_nn(act, buf2[:, span])
    inp = dot_nt(grd, buf1[span, :])
    if not first:
        out = out + out_in[...]
        inp = inp + in_in[...]
    out_o[...] = out.astype(out_o.dtype)
    in_o[...] = inp.astype(in_o.dtype)


def down_call(sizes, width, base, tabs, vals, acts, sums, last):
    total = sum(sizes)
    tokens = acts[0].shape[1]
    first = sums is None
    pair = 2 if width % 2 == 0 else 1
    dtype = jnp.bfloat16 if last else jnp.float32
    acc = pl.BlockSpec((tokens, pair * BLK), lambda i: (0, i))
    shape = jax.ShapeDtypeStruct((tokens, width * BLK), dtype)
    return pl.pallas_call(
        functools.partial(down_kernel, sizes, width, first, last),
        grid=(width // pair,),
        out_shape=[shape, shape],
        in_specs=[smem()] * 3 + [hbm()] * 2 + [vmem()] * len(sizes) + ([] if first else [acc, acc]),
        out_specs=[acc, acc],
        scratch_shapes=tile_scratch(total, width),
        compiler_params=pltpu.CompilerParams(
            vmem_limit_bytes=VMEM_LIMIT, dimension_semantics=("arbitrary",)
        ),
        cost_estimate=pl.CostEstimate(
            flops=4 * tokens * width * total * BLK * BLK,
            bytes_accessed=4 * width * total * BLK * BLK + 16 * tokens * width * BLK,
            transcendentals=0,
        ),
        name="down",
    )(base, *tabs, *vals, *acts, *(() if first else sums))


def grad_kernel(sizes, width, *refs):
    base, tab1, tab2, x_t, dy = refs[:5]
    refs = refs[5:]
    n = len(sizes)
    acts, refs = refs[:n], refs[n:]
    _, _, first_o, second_o, act_t, stage1, stage2, sems = refs
    total = sum(sizes)
    rows = []
    for g, size in enumerate(sizes):
        for k in range(size):
            rows.append((base[g] + k) * width)
    act = jnp.concatenate([a[0] for a in acts], axis=1)
    act_t[...] = act.T
    pairs = (total + 1) // 2
    where = [(g, k) for g, size in enumerate(sizes) for k in range(size)]

    def copies(part, which, b, at, r, go):
        tab = tab1 if which == 0 else tab2
        out = first_o if which == 0 else second_o
        stage = stage1 if which == 0 else stage2
        slot = tab[rows[b] + r]

        @pl.when(slot >= 0)
        def _():
            copy = pltpu.make_async_copy(
                stage.at[part, at], out.at[jnp.maximum(slot, 0)], sems.at[which, part, at]
            )
            if go:
                copy.start()
            else:
                copy.wait()

    plan1 = []
    for p in range(pairs):
        plan1.append([b for b in (2 * p, 2 * p + 1) if b < total])

    def sweep1(p, go):
        for i, b in enumerate(plan1[p]):
            for r in range(width):
                copies(p % 2, 0, b, i * width + r, r, go)

    for p in range(pairs):
        blocks = plan1[p]
        hid = jnp.concatenate(
            [acts[where[b][0]][1, :, where[b][1] * BLK : (where[b][1] + 1) * BLK] for b in blocks], axis=1
        )
        res = dot_nn(x_t[...], hid).astype(jnp.bfloat16)
        if p >= 2:
            sweep1(p - 2, False)
        for i in range(len(blocks)):
            for r in range(width):
                stage1[p % 2, i * width + r] = res[r * BLK : (r + 1) * BLK, i * BLK : (i + 1) * BLK]
        sweep1(p, True)
    span = 2 if width % 2 == 0 else 1
    steps = width // span

    def sweep2(p, go):
        for b in range(total):
            for i in range(span):
                copies(p % 2, 1, b, b * span + i, p * span + i, go)

    for p in range(steps):
        res = dot_nn(act_t[...], dy[:, p * span * BLK : (p + 1) * span * BLK]).astype(jnp.bfloat16)
        if p >= 2:
            sweep2(p - 2, False)
        for b in range(total):
            for i in range(span):
                stage2[p % 2, b * span + i] = res[b * BLK : (b + 1) * BLK, i * BLK : (i + 1) * BLK]
        sweep2(p, True)
    for p in range(max(0, pairs - 2), pairs):
        sweep1(p, False)
    for p in range(max(0, steps - 2), steps):
        sweep2(p, False)


def grad_call(sizes, width, base, tabs, x_t, dy, acts, grads):
    total = sum(sizes)
    tokens = dy.shape[0]
    span = 2 if width % 2 == 0 else 1
    n_stage = max(2 * width, total * span)
    shape = jax.ShapeDtypeStruct(grads[0].shape, jnp.bfloat16)
    n = len(sizes)
    return pl.pallas_call(
        functools.partial(grad_kernel, sizes, width),
        out_shape=[shape, shape],
        in_specs=[smem()] * 3 + [vmem()] * (2 + n) + [hbm()] * 2,
        out_specs=[hbm(), hbm()],
        scratch_shapes=[
            pltpu.VMEM((total * BLK, tokens), jnp.bfloat16),
            pltpu.VMEM((2, n_stage, BLK, BLK), jnp.bfloat16),
            pltpu.VMEM((2, n_stage, BLK, BLK), jnp.bfloat16),
            pltpu.SemaphoreType.DMA((2, 2, n_stage)),
        ],
        input_output_aliases={5 + n: 0, 6 + n: 1},
        compiler_params=pltpu.CompilerParams(vmem_limit_bytes=VMEM_LIMIT),
        cost_estimate=pl.CostEstimate(
            flops=4 * tokens * width * total * BLK * BLK,
            bytes_accessed=4 * width * total * BLK * BLK // 2 + 8 * tokens * width * BLK,
            transcendentals=0,
        ),
        name="grads",
    )(base, *tabs, x_t, dy, *acts, *grads)


def shards(
    inputs,
    out_grad,
    first_vals,
    first_rows,
    first_cols,
    first_count,
    second_vals,
    second_rows,
    second_cols,
    second_count,
    *,
    hidden_blocks,
):
    n = lax.axis_size("col")
    ring = ring_of(n)
    ahead = [(ring[k], ring[(k + 1) % n]) for k in range(n)]
    back = [(b, a) for a, b in ahead]
    place = [0] * n
    for k, dev in enumerate(ring):
        place[dev] = k
    me = jnp.asarray(place, jnp.int32)[lax.axis_index("col")]

    x = lax.all_gather(inputs, "row", axis=0, tiled=True)
    dy = lax.all_gather(out_grad, "row", axis=0, tiled=True)
    width = x.shape[1] // BLK
    per = hidden_blocks // n
    vals = (first_vals[0, 0], second_vals[0, 0])
    n_blocks = hidden_blocks * width
    tabs = (
        block_table(first_cols[0, 0], first_rows[0, 0], first_count[0, 0], width, n_blocks),
        block_table(second_rows[0, 0], second_cols[0, 0], second_count[0, 0], width, n_blocks),
    )

    n_ahead = (per + 1) // 2
    parts = []
    for lo, cnt, sign in ((0, n_ahead, 1), (n_ahead, per - n_ahead, -1)):
        half = (cnt + 1) // 2
        parts.append([(lo, half, sign), (lo + half, cnt - half, sign)])
    streams = [[part[s] for part in parts if part[s][1] > 0] for s in range(2)]
    streams = [s for s in streams if s]

    def bases(stream, shift):
        return jnp.stack([((me - sign * shift) % n) * per + lo for lo, _, sign in stream])

    def hop(stream, arrays):
        return [
            lax.ppermute(a, "col", ahead if sign > 0 else back) for a, (_, _, sign) in zip(arrays, stream)
        ]

    held = [None] * len(streams)
    for t in range(n):
        for s, stream in enumerate(streams):
            sizes = tuple(c for _, c, _ in stream)
            ins = None if t == 0 else hop(stream, held[s])
            held[s] = up_call(sizes, width, bases(stream, t + 1), tabs, x, dy, vals, ins, t == n - 1)

    x_t = x.T
    grads = (jnp.zeros_like(vals[0]), jnp.zeros_like(vals[1]))
    sums = None
    for t in range(n):
        for s, stream in enumerate(streams):
            sizes = tuple(c for _, c, _ in stream)
            if t > 0:
                held[s] = hop(stream, held[s])
            base = bases(stream, t)
            last = t == n - 1 and s == len(streams) - 1
            sums = down_call(sizes, width, base, tabs, vals, held[s], sums, last)
            grads = grad_call(sizes, width, base, tabs, x_t, dy, held[s], grads)

    out_sum = lax.psum_scatter(sums[0], "row", scatter_dimension=0, tiled=True)
    in_sum = lax.psum_scatter(sums[1], "row", scatter_dimension=0, tiled=True)
    return out_sum, in_sum, grads[0][None, None], grads[1][None, None]


def solution(mesh):
    hidden_blocks = 49152 // BLK // mesh.shape["row"]
    placed = (
        P("row", "col"),
        P("row", "col"),
        P("row", "col", None, None, None),
        P("row", "col", None),
        P("row", "col", None),
        P("row", "col"),
        P("row", "col", None, None, None),
        P("row", "col", None),
        P("row", "col", None),
        P("row", "col"),
    )
    return jax.shard_map(
        functools.partial(shards, hidden_blocks=hidden_blocks),
        mesh=mesh,
        in_specs=placed,
        out_specs=(
            P("row", "col"),
            P("row", "col"),
            P("row", "col", None, None, None),
            P("row", "col", None, None, None),
        ),
        check_vma=False,
    )
```

```python
import functools

import jax
import jax.numpy as jnp
from jax import lax
from jax.experimental import pallas as pl
from jax.experimental.pallas import tpu as pltpu
from jax.sharding import PartitionSpec as P

BLK = 128
Z_CHIPS = 4
ROOT_2_PI = 0.7978845608028654
CUBIC = 0.044715
VMEM_LIMIT = 48 << 20
FIRST_SHIFT = 20
SECOND_SHIFT = 14


def ring_of(n):
    if n % Z_CHIPS or n // Z_CHIPS < 2:
        return list(range(n))
    wide = n // Z_CHIPS
    order = [z * wide for z in range(Z_CHIPS)]
    for k, z in enumerate(reversed(range(Z_CHIPS))):
        ys = range(1, wide) if k % 2 == 0 else range(wide - 1, 0, -1)
        order += [z * wide + y for y in ys]
    return order


def gelu_pair(value, grad):
    inner = ROOT_2_PI * (value + CUBIC * (value * value * value))
    th = jnp.tanh(inner)
    half = 0.5 * (1.0 + th)
    slope = half + 0.5 * value * (1.0 - th * th) * (ROOT_2_PI * (1.0 + (3.0 * CUBIC) * (value * value)))
    return value * half, grad * slope


def slot_order(first, second, count, n_first):
    slots = first.shape[0]
    ids = jnp.arange(slots, dtype=jnp.int32)
    packed = (first << FIRST_SHIFT) | (second << SECOND_SHIFT) | ids
    key = jnp.where(ids < count, packed, jnp.iinfo(jnp.int32).max - slots + ids)
    rank = jnp.sum((key[None, :] < key[:, None]).astype(jnp.int32), axis=1)
    order = jnp.sum(jnp.where(rank[None, :] == ids[:, None], packed[None, :], 0), axis=1)
    edge = jnp.arange(n_first + 1, dtype=jnp.int32) << FIRST_SHIFT
    starts = jnp.sum((key[None, :] < edge[:, None]).astype(jnp.int32), axis=1)
    return starts, order


class Plan:
    def __init__(self, stream, shift, n, per, hidden_blocks, slots, width):
        self.stream, self.shift, self.n, self.per = tuple(stream), shift, n, per
        self.sizes = tuple(c for _, c, _ in stream)
        self.total = sum(self.sizes)
        self.width = width
        self.tokens = None
        self.start_at = (1, 2 + hidden_blocks)
        self.list_at = (3 + 2 * hidden_blocks, 3 + 2 * hidden_blocks + slots)

    def bases(self, meta):
        me = meta[0]
        return [lax.rem(me + (self.n - sign * self.shift) % self.n, self.n) * self.per + lo for lo, _, sign in self.stream]

    def each(self, meta, which, body):
        offset = 0
        for base, size in zip(self.bases(meta), self.sizes):
            lo = meta[self.start_at[which] + base]
            hi = meta[self.start_at[which] + base + size]

            def step(i, carry, base=base, offset=offset):
                entry = meta[self.list_at[which] + i]
                slot = entry & ((1 << SECOND_SHIFT) - 1)
                r = (entry >> SECOND_SHIFT) & ((1 << (FIRST_SHIFT - SECOND_SHIFT)) - 1)
                body(slot, (entry >> FIRST_SHIFT) - base + offset, r)
                return carry

            lax.fori_loop(lo, hi, step, 0)
            offset += size


def block_at(i):
    return pl.ds(pl.multiple_of(i * BLK, BLK), BLK)


def clear(buf):
    def step(i, carry):
        buf[block_at(i), :] = jnp.zeros((BLK, buf.shape[1]), buf.dtype)
        return carry

    lax.fori_loop(0, buf.shape[0] // BLK, step, 0)


def tile_start(plan, meta, vals, buf, sems, which):
    clear(buf)

    def go(slot, b, r):
        dst = buf.at[block_at(r), block_at(b)] if which == 0 else buf.at[block_at(b), block_at(r)]
        pltpu.make_async_copy(vals.at[slot], dst, sems.at[which, b, r]).start()

    plan.each(meta, which, go)


def tile_wait(plan, meta, vals, buf, sems, which):
    def go(slot, b, r):
        pltpu.make_async_copy(vals.at[slot], buf.at[pl.ds(0, BLK), pl.ds(0, BLK)], sems.at[which, b, r]).wait()

    plan.each(meta, which, go)


def dot_nn(a, b):
    return jnp.dot(a, b, preferred_element_type=jnp.float32)


def dot_nt(a, b):
    return lax.dot_general(a, b, (((1,), (1,)), ((), ())), preferred_element_type=jnp.float32)


def spans(plan):
    where = [(g, k) for g, size in enumerate(plan.sizes) for k in range(size)]
    return [(lo, where[lo : lo + 2]) for lo in range(0, plan.total, 2)]


def up_kernel(plan, has_in, last, *refs):
    meta, x, dy, vals1, vals2 = refs[:5]
    refs = refs[5:]
    n = len(plan.sizes)
    ins = refs[:n] if has_in else None
    refs = refs[n:] if has_in else refs
    outs, refs = refs[:n], refs[n:]
    if last:
        hid_ref, refs = refs[0], refs[1:]
    buf1, buf2, sems = refs
    tile_start(plan, meta, vals1, buf1, sems, 0)
    tile_start(plan, meta, vals2, buf2, sems, 1)
    tile_wait(plan, meta, vals1, buf1, sems, 0)
    for lo, pair in spans(plan):
        res = dot_nn(x[...], buf1[:, lo * BLK : (lo + len(pair)) * BLK])
        for i, (g, k) in enumerate(pair):
            at = slice(k * BLK, (k + 1) * BLK)
            h = res[:, i * BLK : (i + 1) * BLK]
            if has_in:
                h = h + ins[g][0, :, at].astype(jnp.float32)
            if last:
                hid_ref[:, (lo + i) * BLK : (lo + i + 1) * BLK] = h
            else:
                outs[g][0, :, at] = h.astype(jnp.bfloat16)
    tile_wait(plan, meta, vals2, buf2, sems, 1)
    for lo, pair in spans(plan):
        res = dot_nt(dy[...], buf2[lo * BLK : (lo + len(pair)) * BLK, :])
        for i, (g, k) in enumerate(pair):
            at = slice(k * BLK, (k + 1) * BLK)
            d = res[:, i * BLK : (i + 1) * BLK]
            if has_in:
                d = d + ins[g][1, :, at].astype(jnp.float32)
            if last:
                act, d = gelu_pair(hid_ref[:, (lo + i) * BLK : (lo + i + 1) * BLK], d)
                outs[g][0, :, at] = act.astype(jnp.bfloat16)
            outs[g][1, :, at] = d.astype(jnp.bfloat16)


def smem():
    return pl.BlockSpec(memory_space=pltpu.SMEM)


def vmem():
    return pl.BlockSpec(memory_space=pltpu.VMEM)


def hbm():
    return pl.BlockSpec(memory_space=pltpu.HBM)


def tile_scratch(total, width):
    return [
        pltpu.VMEM((width * BLK, total * BLK), jnp.bfloat16),
        pltpu.VMEM((total * BLK, width * BLK), jnp.bfloat16),
        pltpu.SemaphoreType.DMA((2, total, width)),
    ]


def up_call(plan, meta, x, dy, vals, ins, last):
    tokens = x.shape[0]
    n = len(plan.sizes)
    has_in = ins is not None
    total, width = plan.total, plan.width
    return pl.pallas_call(
        functools.partial(up_kernel, plan, has_in, last),
        out_shape=[jax.ShapeDtypeStruct((2, tokens, s * BLK), jnp.bfloat16) for s in plan.sizes],
        in_specs=[smem()] + [vmem()] * 2 + [hbm()] * 2 + [vmem()] * (n if has_in else 0),
        out_specs=[vmem()] * n,
        scratch_shapes=([pltpu.VMEM((tokens, total * BLK), jnp.float32)] if last else [])
        + tile_scratch(total, width),
        compiler_params=pltpu.CompilerParams(vmem_limit_bytes=VMEM_LIMIT),
        cost_estimate=pl.CostEstimate(
            flops=4 * tokens * width * total * BLK * BLK,
            bytes_accessed=4 * width * total * BLK * BLK + 8 * tokens * total * BLK,
            transcendentals=0,
        ),
        name="up_last" if last else "up",
    )(meta, x, dy, *vals, *(ins if has_in else ()))


def down_kernel(plan, first, last, *refs):
    meta, vals1, vals2 = refs[:3]
    refs = refs[3:]
    n = len(plan.sizes)
    acts, refs = refs[:n], refs[n:]
    if not first:
        olds, refs = refs[:2], refs[2:]
    n_out = 4 if last else 2
    outs, refs = refs[:n_out], refs[n_out:]
    act, grd, buf1, buf2, sems = refs
    tile_start(plan, meta, vals2, buf2, sems, 1)
    tile_start(plan, meta, vals1, buf1, sems, 0)
    at = 0
    for a, size in zip(acts, plan.sizes):
        act[:, at : at + size * BLK] = a[0]
        grd[:, at : at + size * BLK] = a[1]
        at += size * BLK
    tokens = act.shape[0]
    columns = plan.width * BLK
    wide = 256 if columns % 256 == 0 else BLK
    for which in (1, 0):
        tile_wait(plan, meta, (vals1, vals2)[which], (buf1, buf2)[which], sems, which)
        for lo in range(0, columns, wide):
            span = slice(lo, lo + wide)
            if which == 1:
                res = dot_nn(act[...], buf2[:, span])
            else:
                res = dot_nt(grd[...], buf1[span, :])
            k = 1 - which
            if not first:
                res = res + olds[k][:, span]
            if last:
                outs[2 * k][:, span] = res[: tokens // 2]
                outs[2 * k + 1][:, span] = res[tokens // 2 :].astype(jnp.bfloat16)
            else:
                outs[k][:, span] = res


def down_call(plan, meta, vals, acts, sums, last):
    total, width = plan.total, plan.width
    tokens = acts[0].shape[1]
    first = sums is None
    n = len(plan.sizes)
    if last:
        shapes = [
            jax.ShapeDtypeStruct((tokens // 2, width * BLK), jnp.float32),
            jax.ShapeDtypeStruct((tokens // 2, width * BLK), jnp.bfloat16),
        ] * 2
    else:
        shapes = [jax.ShapeDtypeStruct((tokens, width * BLK), jnp.float32)] * 2
    return pl.pallas_call(
        functools.partial(down_kernel, plan, first, last),
        out_shape=shapes,
        in_specs=[smem()] + [hbm()] * 2 + [vmem()] * (n if first else n + 2),
        out_specs=[vmem()] * len(shapes),
        input_output_aliases={} if first or last else {3 + n: 0, 4 + n: 1},
        scratch_shapes=[pltpu.VMEM((tokens, total * BLK), jnp.bfloat16)] * 2 + tile_scratch(total, width),
        compiler_params=pltpu.CompilerParams(vmem_limit_bytes=VMEM_LIMIT),
        cost_estimate=pl.CostEstimate(
            flops=4 * tokens * width * total * BLK * BLK,
            bytes_accessed=4 * width * total * BLK * BLK,
            transcendentals=0,
        ),
        name="down",
    )(meta, *vals, *acts, *(() if first else sums))


def grad_kernel(plan, *refs):
    meta, x_t, dy = refs[:3]
    refs = refs[3:]
    n = len(plan.sizes)
    acts, refs = refs[:n], refs[n:]
    _, _, first_o, second_o, grd, act_t, stage1, stage2, sems = refs
    at = 0
    for a, size in zip(acts, plan.sizes):
        act_t[at : at + size * BLK, :] = a[0].T
        grd[:, at : at + size * BLK] = a[1]
        at += size * BLK
    outs, stages = (first_o, second_o), (stage1, stage2)

    def send(which):
        def go(slot, b, r):
            src = stage1.at[block_at(r), block_at(b)] if which == 0 else stage2.at[block_at(b), block_at(r)]
            pltpu.make_async_copy(src, outs[which].at[slot], sems.at[which, b, r]).start()

        plan.each(meta, which, go)

    def drain(which):
        def go(slot, b, r):
            src = stages[which].at[pl.ds(0, BLK), pl.ds(0, BLK)]
            pltpu.make_async_copy(src, outs[which].at[slot], sems.at[which, b, r]).wait()

        plan.each(meta, which, go)

    for lo, pair in spans(plan):
        span = slice(lo * BLK, (lo + len(pair)) * BLK)
        stage1[:, span] = dot_nn(x_t[...], grd[:, span]).astype(jnp.bfloat16)
    send(0)
    columns = plan.width * BLK
    wide = 256 if columns % 256 == 0 else BLK
    for lo in range(0, columns, wide):
        stage2[:, lo : lo + wide] = dot_nn(act_t[...], dy[:, lo : lo + wide]).astype(jnp.bfloat16)
    send(1)
    drain(0)
    drain(1)


def grad_call(plan, meta, x_t, dy, acts, grads):
    total, width = plan.total, plan.width
    tokens = dy.shape[0]
    shape = jax.ShapeDtypeStruct(grads[0].shape, jnp.bfloat16)
    n = len(plan.sizes)
    return pl.pallas_call(
        functools.partial(grad_kernel, plan),
        out_shape=[shape, shape],
        in_specs=[smem()] + [vmem()] * (2 + n) + [hbm()] * 2,
        out_specs=[hbm(), hbm()],
        scratch_shapes=[
            pltpu.VMEM((tokens, total * BLK), jnp.bfloat16),
            pltpu.VMEM((total * BLK, tokens), jnp.bfloat16),
        ]
        + tile_scratch(total, width),
        input_output_aliases={3 + n: 0, 4 + n: 1},
        compiler_params=pltpu.CompilerParams(vmem_limit_bytes=VMEM_LIMIT),
        cost_estimate=pl.CostEstimate(
            flops=4 * tokens * width * total * BLK * BLK,
            bytes_accessed=2 * width * total * BLK * BLK,
            transcendentals=0,
        ),
        name="grads",
    )(meta, x_t, dy, *acts, *grads)


class Row:
    def __init__(self, size):
        self.cores = 2 if size % 2 == 0 else 1
        self.chips = size // self.cores

    def swap(self, value):
        if self.cores == 1:
            return value
        return lax.ppermute(value, "row", [(k, k ^ 1) for k in range(self.chips * 2)])

    def shift(self, value, step):
        pairs = []
        for x in range(self.chips):
            for c in range(self.cores):
                pairs.append((((x + step) % self.chips) * self.cores + c, x * self.cores + c))
        return lax.ppermute(value, "row", pairs)

    def gather(self, value):
        half = jnp.concatenate([value] + [self.shift(value, d) for d in range(1, self.chips)], axis=0)
        return jnp.concatenate([half, self.swap(half)], axis=0)

    def scatter(self, keep, send):
        total = keep + self.swap(send).astype(jnp.float32)
        rows = total.shape[0] // self.chips
        mine = total[:rows]
        for d in range(1, self.chips):
            part = total[d * rows : (d + 1) * rows].astype(jnp.bfloat16)
            mine = mine + self.shift(part, -d).astype(jnp.float32)
        return mine.astype(jnp.bfloat16)


def shards(
    inputs,
    out_grad,
    first_vals,
    first_rows,
    first_cols,
    first_count,
    second_vals,
    second_rows,
    second_cols,
    second_count,
    *,
    hidden_blocks,
):
    n = lax.axis_size("col")
    ring = ring_of(n)
    ahead = [(ring[k], ring[(k + 1) % n]) for k in range(n)]
    back = [(b, a) for a, b in ahead]
    place = [0] * n
    for k, dev in enumerate(ring):
        place[dev] = k
    me = jnp.asarray(place, jnp.int32)[lax.axis_index("col")]

    row = Row(lax.axis_size("row"))
    x = row.gather(inputs)
    dy = row.gather(out_grad)
    width = x.shape[1] // BLK
    per = hidden_blocks // n
    vals = (first_vals[0, 0], second_vals[0, 0])
    slots = vals[0].shape[0]
    starts1, order1 = slot_order(first_cols[0, 0], first_rows[0, 0], first_count[0, 0], hidden_blocks)
    starts2, order2 = slot_order(second_rows[0, 0], second_cols[0, 0], second_count[0, 0], hidden_blocks)
    meta = jnp.concatenate([me[None], starts1, starts2, order1, order2])

    n_ahead = (per + 1) // 2
    parts = []
    for lo, cnt, sign in ((0, n_ahead, 1), (n_ahead, per - n_ahead, -1)):
        half = (cnt + 1) // 2
        parts.append([(lo, half, sign), (lo + half, cnt - half, sign)])
    streams = [[part[s] for part in parts if part[s][1] > 0] for s in range(2)]
    streams = [s for s in streams if s]

    def plan_of(stream, shift):
        return Plan(stream, shift, n, per, hidden_blocks, slots, width)

    def hop(stream, arrays):
        return [
            lax.ppermute(a, "col", ahead if sign > 0 else back) for a, (_, _, sign) in zip(arrays, stream)
        ]

    held = [None] * len(streams)
    x_t = grads = None
    for t in range(n):
        for s, stream in enumerate(streams):
            ins = None if t == 0 else hop(stream, held[s])
            if t == 1 and s == 0:
                x_t = x.T
                ins, x_t = lax.optimization_barrier((ins, x_t))
            if t == 2 and s == 0:
                grads = (jnp.zeros_like(vals[0]), jnp.zeros_like(vals[1]))
                ins, grads = lax.optimization_barrier((ins, grads))
            held[s] = up_call(plan_of(stream, t + 1), meta, x, dy, vals, ins, t == n - 1)

    sums = None
    for t in range(n):
        for s, stream in enumerate(streams):
            if t > 0:
                held[s] = hop(stream, held[s])
                held[s], sums, grads = lax.optimization_barrier((held[s], sums, grads))
            last = t == n - 1 and s == len(streams) - 1
            plan = plan_of(stream, t)
            sums = down_call(plan, meta, vals, held[s], sums, last)
            grads = grad_call(plan, meta, x_t, dy, held[s], grads)

    out_sum = row.scatter(sums[0], sums[1])
    in_sum = row.scatter(sums[2], sums[3])
    return out_sum, in_sum, grads[0][None, None], grads[1][None, None]


def solution(mesh):
    hidden_blocks = 49152 // BLK // mesh.shape["row"]
    placed = (
        P("row", "col"),
        P("row", "col"),
        P("row", "col", None, None, None),
        P("row", "col", None),
        P("row", "col", None),
        P("row", "col"),
        P("row", "col", None, None, None),
        P("row", "col", None),
        P("row", "col", None),
        P("row", "col"),
    )
    return jax.shard_map(
        functools.partial(shards, hidden_blocks=hidden_blocks),
        mesh=mesh,
        in_specs=placed,
        out_specs=(
            P("row", "col"),
            P("row", "col"),
            P("row", "col", None, None, None),
            P("row", "col", None, None, None),
        ),
        check_vma=False,
    )
```

```python
import functools

import jax
import jax.numpy as jnp
from jax import lax
from jax.experimental import pallas as pl
from jax.experimental.pallas import tpu as pltpu
from jax.sharding import PartitionSpec as P

BLK = 128
Z_CHIPS = 4
ROOT_2_PI = 0.7978845608028654
CUBIC = 0.044715
VMEM_LIMIT = 40 << 20
FIRST_LIMIT = 60 << 20
FIRST_SHIFT = 20
SECOND_SHIFT = 14


def ring_of(n):
    if n % Z_CHIPS or n // Z_CHIPS < 2:
        return list(range(n))
    wide = n // Z_CHIPS
    order = [z * wide for z in range(Z_CHIPS)]
    for k, z in enumerate(reversed(range(Z_CHIPS))):
        ys = range(1, wide) if k % 2 == 0 else range(wide - 1, 0, -1)
        order += [z * wide + y for y in ys]
    return order


def gelu_pair(value, grad):
    inner = ROOT_2_PI * (value + CUBIC * (value * value * value))
    th = jnp.tanh(inner)
    half = 0.5 * (1.0 + th)
    slope = half + 0.5 * value * (1.0 - th * th) * (ROOT_2_PI * (1.0 + (3.0 * CUBIC) * (value * value)))
    return value * half, grad * slope


def slot_order(first, second, count, n_first):
    slots = first.shape[0]
    ids = jnp.arange(slots, dtype=jnp.int32)
    packed = (first << FIRST_SHIFT) | (second << SECOND_SHIFT) | ids
    key = jnp.where(ids < count, packed, jnp.iinfo(jnp.int32).max - slots + ids)
    rank = jnp.sum((key[None, :] < key[:, None]).astype(jnp.int32), axis=1)
    order = jnp.sum(jnp.where(rank[None, :] == ids[:, None], packed[None, :], 0), axis=1)
    edge = jnp.arange(n_first + 1, dtype=jnp.int32) << FIRST_SHIFT
    starts = jnp.sum((key[None, :] < edge[:, None]).astype(jnp.int32), axis=1)
    return starts, order


class Plan:
    def __init__(self, stream, shift, n, per, hidden_blocks, slots, width, parts=()):
        self.stream, self.shift, self.n, self.per = tuple(stream), shift, n, per
        self.sizes = tuple(c for _, c, _ in stream)
        self.total = sum(self.sizes)
        self.width = width
        self.parts = tuple(parts) if parts else (self,)
        self.start_at = (1, 2 + hidden_blocks)
        self.list_at = (3 + 2 * hidden_blocks, 3 + 2 * hidden_blocks + slots)

    def bases(self, meta):
        me = meta[0]
        return [lax.rem(me + (self.n - sign * self.shift) % self.n, self.n) * self.per + lo for lo, _, sign in self.stream]

    def each(self, meta, which, body):
        offset = 0
        for base, size in zip(self.bases(meta), self.sizes):
            lo = meta[self.start_at[which] + base]
            hi = meta[self.start_at[which] + base + size]

            def step(i, carry, base=base, offset=offset):
                entry = meta[self.list_at[which] + i]
                slot = entry & ((1 << SECOND_SHIFT) - 1)
                r = (entry >> SECOND_SHIFT) & ((1 << (FIRST_SHIFT - SECOND_SHIFT)) - 1)
                body(slot, (entry >> FIRST_SHIFT) - base + offset, r)
                return carry

            lax.fori_loop(lo, hi, step, 0)
            offset += size


def block_at(i):
    return pl.ds(pl.multiple_of(i * BLK, BLK), BLK)


def clear(buf):
    def step(i, carry):
        buf[block_at(i), :] = jnp.zeros((BLK, buf.shape[1]), buf.dtype)
        return carry

    lax.fori_loop(0, buf.shape[0] // BLK, step, 0)


def tile_start(plan, meta, vals, buf, sems, which):
    clear(buf)

    def go(slot, b, r):
        dst = buf.at[block_at(r), block_at(b)] if which == 0 else buf.at[block_at(b), block_at(r)]
        pltpu.make_async_copy(vals.at[slot], dst, sems.at[which, b, r]).start()

    plan.each(meta, which, go)


def tile_wait(plan, meta, vals, buf, sems, which):
    def go(slot, b, r):
        pltpu.make_async_copy(vals.at[slot], buf.at[pl.ds(0, BLK), pl.ds(0, BLK)], sems.at[which, b, r]).wait()

    plan.each(meta, which, go)


def dot_nn(a, b):
    return jnp.dot(a, b, preferred_element_type=jnp.float32)


def dot_nt(a, b):
    return lax.dot_general(a, b, (((1,), (1,)), ((), ())), preferred_element_type=jnp.float32)


def tile_loop(columns, body):
    wide = 2 * BLK if columns % (2 * BLK) == 0 else BLK
    if columns == wide:
        body(pl.ds(0, wide))
        return

    def step(i, carry):
        body(pl.ds(pl.multiple_of(i * wide, wide), wide))
        return carry

    lax.fori_loop(0, columns // wide, step, 0)


def row_loop(rows, body):
    def step(i, carry):
        body(block_at(i))
        return carry

    lax.fori_loop(0, rows // BLK, step, 0)


def group_slices(plan):
    at, out = 0, []
    for size in plan.sizes:
        out.append(slice(at, at + size * BLK))
        at += size * BLK
    return out


class Store:
    def __init__(self, plan):
        self.side, self.rows = plan.total * BLK, plan.width * BLK
        self.cuts = plan.width // plan.total
        self.shape = (plan.n, 2 * self.rows, self.side)

    def views(self, store, step, which, buf):
        if which == 0:
            return [(store.at[step, pl.ds(0, self.rows), :], buf)]
        return [
            (store.at[step, pl.ds(self.rows + i * self.side, self.side), :], buf.at[:, pl.ds(i * self.side, self.side)])
            for i in range(self.cuts)
        ]


def up_kernel(plan, n_pieces, has_in, last, *refs):
    meta, refs = refs[0], refs[1:]
    if n_pieces:
        pieces, refs = refs[: 2 * n_pieces], refs[2 * n_pieces :]
    else:
        x, dy, refs = refs[0], refs[1], refs[2:]
    vals1, vals2, refs = refs[0], refs[1], refs[2:]
    n = len(plan.sizes)
    ins = refs[:n] if has_in else None
    refs = refs[n + 1 :] if has_in else refs
    outs, refs = refs[:n], refs[n:]
    if n_pieces:
        x, dy, refs = refs[0], refs[1], refs[2:]
    store, refs = refs[0], refs[1:]
    buf1, buf2, sems, hid, grd, tile_sems = refs[:6]
    keep = [
        [
            pltpu.make_async_copy(src, dst, tile_sems.at[which, i])
            for i, (dst, src) in enumerate(Store(plan).views(store, plan.shift - 1, which, buf))
        ]
        for which, buf in enumerate((buf1, buf2))
    ]
    joins = []
    if n_pieces:
        rows = pieces[0].shape[0]
        for i in range(2 * n_pieces):
            dst = (x if i < n_pieces else dy).at[pl.ds(i % n_pieces * rows, rows), :]
            joins.append(pltpu.make_async_copy(pieces[i], dst, refs[6].at[i]))
    for join in joins:
        join.start()
    tile_start(plan, meta, vals1, buf1, sems, 0)
    tile_start(plan, meta, vals2, buf2, sems, 1)
    for join in joins:
        join.wait()
    columns = plan.total * BLK
    tile_wait(plan, meta, vals1, buf1, sems, 0)
    for copy in keep[0]:
        copy.start()

    def hid_tile(at):
        hid[:, at] = dot_nn(x[...], buf1[:, at])

    tile_loop(columns, hid_tile)
    tile_wait(plan, meta, vals2, buf2, sems, 1)
    for copy in keep[1]:
        copy.start()

    def grd_tile(at):
        grd[:, at] = dot_nt(dy[...], buf2[at, :])

    tile_loop(columns, grd_tile)

    def join_rows(part):
        for g, at in enumerate(group_slices(plan)):
            h, d = hid[part, at], grd[part, at]
            if has_in:
                h = h + ins[g][0, part, :].astype(jnp.float32)
                d = d + ins[g][1, part, :].astype(jnp.float32)
            if last:
                h, d = gelu_pair(h, d)
            outs[g][0, part, :] = h.astype(jnp.bfloat16)
            outs[g][1, part, :] = d.astype(jnp.bfloat16)

    row_loop(hid.shape[0], join_rows)
    for copy in keep[0] + keep[1]:
        copy.wait()


def smem():
    return pl.BlockSpec(memory_space=pltpu.SMEM)


def vmem():
    return pl.BlockSpec(memory_space=pltpu.VMEM)


def hbm():
    return pl.BlockSpec(memory_space=pltpu.HBM)


def tile_scratch(total, width):
    return [
        pltpu.VMEM((width * BLK, total * BLK), jnp.bfloat16),
        pltpu.VMEM((total * BLK, width * BLK), jnp.bfloat16),
        pltpu.SemaphoreType.DMA((2, total, width)),
    ]


def up_call(plan, meta, x, dy, vals, ins, store, last):
    pieces = isinstance(x, list)
    n_pieces = len(x) if pieces else 0
    given = (*x, *dy) if pieces else (x, dy)
    tokens = sum(p.shape[0] for p in x) if pieces else x.shape[0]
    n = len(plan.sizes)
    has_in = ins is not None
    total, width = plan.total, plan.width
    shapes = [jax.ShapeDtypeStruct((2, tokens, s * BLK), jnp.bfloat16) for s in plan.sizes]
    if pieces:
        shapes += [jax.ShapeDtypeStruct((tokens, width * BLK), jnp.bfloat16)] * 2
    in_vmem = len(shapes)
    shapes.append(jax.ShapeDtypeStruct(Store(plan).shape, jnp.bfloat16))
    n_in = 3 + len(given) + n
    res = pl.pallas_call(
        functools.partial(up_kernel, plan, n_pieces, has_in, last),
        out_shape=shapes,
        in_specs=[smem()]
        + [hbm() if pieces else vmem()] * len(given)
        + [hbm()] * 2
        + ([vmem()] * n + [hbm()] if has_in else []),
        out_specs=[vmem()] * in_vmem + [hbm()],
        input_output_aliases={n_in: in_vmem} if has_in else {},
        scratch_shapes=tile_scratch(total, width)
        + [pltpu.VMEM((tokens, total * BLK), jnp.float32)] * 2
        + [pltpu.SemaphoreType.DMA((2, Store(plan).cuts))]
        + ([pltpu.SemaphoreType.DMA((2 * n_pieces,))] if pieces else []),
        compiler_params=pltpu.CompilerParams(vmem_limit_bytes=FIRST_LIMIT if pieces else VMEM_LIMIT),
        cost_estimate=pl.CostEstimate(
            flops=4 * tokens * width * total * BLK * BLK,
            bytes_accessed=4 * width * total * BLK * BLK + 8 * tokens * total * BLK,
            transcendentals=0,
        ),
        name="up_last" if last else "up",
    )(meta, *given, *vals, *((*ins, store) if has_in else ()))
    return (res[:n], res[-1], res[n], res[n + 1]) if pieces else (res[:n], res[-1])


DEAD_GROUP = 16


def dead_kernel(which, plan, slots, meta, out, zeros, sems):
    zeros[...] = jnp.zeros_like(zeros)
    live = meta[plan.start_at[which] + plan.per * plan.n]
    edge = jnp.minimum((live + DEAD_GROUP - 1) // DEAD_GROUP * DEAD_GROUP, slots)

    def one(i):
        return pltpu.make_async_copy(zeros.at[0], out.at[i], sems.at[i % DEAD_GROUP])

    def many(i):
        return pltpu.make_async_copy(
            zeros, out.at[pl.ds(i * DEAD_GROUP, DEAD_GROUP)], sems.at[DEAD_GROUP + i]
        )

    def loop(lo, hi, body):
        def step(i, carry):
            body(i)
            return carry

        lax.fori_loop(lo, hi, step, 0)

    loop(edge // DEAD_GROUP, slots // DEAD_GROUP, lambda i: many(i).start())
    loop(live, edge, lambda i: one(i).start())
    loop(edge // DEAD_GROUP, slots // DEAD_GROUP, lambda i: many(i).wait())
    loop(live, edge, lambda i: one(i).wait())


def dead_call(which, plan, meta, like):
    slots = like.shape[0]
    return pl.pallas_call(
        functools.partial(dead_kernel, which, plan, slots),
        out_shape=jax.ShapeDtypeStruct(like.shape, like.dtype),
        in_specs=[smem()],
        out_specs=hbm(),
        scratch_shapes=[
            pltpu.VMEM((DEAD_GROUP, BLK, BLK), like.dtype),
            pltpu.SemaphoreType.DMA((DEAD_GROUP + slots // DEAD_GROUP,)),
        ],
        compiler_params=pltpu.CompilerParams(vmem_limit_bytes=VMEM_LIMIT),
        cost_estimate=pl.CostEstimate(flops=0, bytes_accessed=slots * BLK * BLK, transcendentals=0),
        name="dead",
    )(meta)


def back_kernel(plan, down, grads, first, last, *refs):
    meta, refs = refs[0], refs[1:]
    if grads:
        x_t, dy, refs = refs[0], refs[1], refs[2:]
    if down:
        stores, refs = refs[: len(plan.parts)], refs[len(plan.parts) :]
    n = len(plan.sizes)
    acts, refs = refs[:n], refs[n:]
    olds, outs = {}, {}
    if not first:
        for k in down:
            olds[k], refs = refs[0], refs[1:]
    if grads:
        refs = refs[2:]
    for k in down:
        outs[k], refs = (refs[:2], refs[2:]) if last else (refs[:1], refs[1:])
    if grads:
        slot_out, refs = refs[:2], refs[2:]
    act, grd = refs[:2]
    if down:
        bufs, sems = dict(zip(down, refs[2 : 2 + len(down)])), refs[2 + len(down)]
    if grads:
        act_t, stage1, stage2, out_sems = refs[-4:]
    tokens = act.shape[0]
    columns = plan.width * BLK
    loads = {}
    for k in down:
        at, loads[k] = 0, []
        for store, part in zip(stores, plan.parts):
            span = pl.ds(at * BLK, part.total * BLK)
            dst = bufs[k].at[span, :] if k == 0 else bufs[k].at[:, span]
            for src, to in Store(part).views(store, (plan.shift - 1) % plan.n, 1 - k, dst):
                loads[k].append(pltpu.make_async_copy(src, to, sems.at[k, len(loads[k])]))
            at += part.total
        for load in loads[k]:
            load.start()

    def split_rows(part):
        for a, at in zip(acts, group_slices(plan)):
            value = a[0, part, :]
            act[part, at] = value
            grd[part, at] = a[1, part, :]
            if grads:
                act_t[at, part] = value.T

    row_loop(tokens, split_rows)

    def block_of(which, b, r):
        if which == 0:
            return stage1.at[block_at(r), block_at(b)]
        return stage2.at[block_at(b), block_at(r)]

    def send(which):
        def go(slot, b, r):
            pltpu.make_async_copy(block_of(which, b, r), slot_out[which].at[slot], out_sems.at[which, b, r]).start()

        plan.each(meta, which, go)

    def drain(which):
        def go(slot, b, r):
            pltpu.make_async_copy(block_of(which, 0, 0), slot_out[which].at[slot], out_sems.at[which, b, r]).wait()

        plan.each(meta, which, go)

    def weigh(k):
        for load in loads[k]:
            load.wait()

        def tile(at):
            res = dot_nn(act[...], bufs[0][:, at]) if k == 0 else dot_nt(grd[...], bufs[1][at, :])
            if not first:
                res = res + olds[k][:, at]
            if last:
                outs[k][0][:, at] = res[: tokens // 2]
                outs[k][1][:, at] = res[tokens // 2 :].astype(jnp.bfloat16)
            else:
                outs[k][0][:, at] = res

        tile_loop(columns, tile)

    if grads:

        def first_tile(at):
            stage1[:, at] = dot_nn(x_t[...], grd[:, at]).astype(jnp.bfloat16)

        tile_loop(plan.total * BLK, first_tile)
        send(0)
    if 0 in down:
        weigh(0)
    if grads:

        def second_tile(at):
            stage2[:, at] = dot_nn(act_t[...], dy[:, at]).astype(jnp.bfloat16)

        tile_loop(columns, second_tile)
        send(1)
    if 1 in down:
        weigh(1)
    if grads:
        drain(0)
        drain(1)


def back_call(plan, meta, x_t, dy, stores, acts, sums, grads, *, down=(0, 1), with_grads=True, last=False):
    total, width = plan.total, plan.width
    tokens = acts[0].shape[1]
    n = len(plan.sizes)
    first = sums is None
    acc = jax.ShapeDtypeStruct((tokens, width * BLK), jnp.float32)
    half = [jax.ShapeDtypeStruct((tokens // 2, width * BLK), t) for t in (jnp.float32, jnp.bfloat16)]
    operands = [meta]
    specs = [smem()]
    if with_grads:
        operands += [x_t, dy]
        specs += [vmem()] * 2
    if down:
        operands += stores
        specs += [hbm()] * len(stores)
    operands += acts
    specs += [vmem()] * n
    shapes, outs, alias = [], [], {}
    for k in down:
        if not first:
            if not last:
                alias[len(operands)] = len(shapes)
            operands.append(sums[k])
            specs.append(vmem())
        shapes += half if last else [acc]
        outs += [vmem()] * (2 if last else 1)
    if with_grads:
        for k in (0, 1):
            alias[len(operands)] = len(shapes)
            operands.append(grads[k])
            specs.append(hbm())
            shapes.append(jax.ShapeDtypeStruct(grads[k].shape, jnp.bfloat16))
            outs.append(hbm())
    scratch = [pltpu.VMEM((tokens, total * BLK), jnp.bfloat16)] * 2
    if down:
        big = tile_scratch(total, width)
        scratch += [big[1 - k] for k in down] + [pltpu.SemaphoreType.DMA((2, sum(Store(p).cuts for p in plan.parts)))]
    if with_grads:
        stage1, stage2, sems = tile_scratch(total, width)
        scratch += [
            pltpu.VMEM((total * BLK, tokens), jnp.bfloat16),
            stage1,
            stage2,
            sems,
        ]
    parts = len(down) + (2 if with_grads else 0)
    return pl.pallas_call(
        functools.partial(back_kernel, plan, down, with_grads, first, last),
        out_shape=shapes,
        in_specs=specs,
        out_specs=outs,
        input_output_aliases=alias,
        scratch_shapes=scratch,
        compiler_params=pltpu.CompilerParams(vmem_limit_bytes=VMEM_LIMIT),
        cost_estimate=pl.CostEstimate(
            flops=2 * parts * tokens * width * total * BLK * BLK,
            bytes_accessed=parts * width * total * BLK * BLK,
            transcendentals=0,
        ),
        name="back",
    )(*operands)


class Row:
    def __init__(self, size):
        self.cores = 2 if size % 2 == 0 else 1
        self.chips = size // self.cores

    def swap(self, value):
        if self.cores == 1:
            return value
        return lax.ppermute(value, "row", [(k, k ^ 1) for k in range(self.chips * 2)])

    def shift(self, value, step):
        pairs = []
        for x in range(self.chips):
            for c in range(self.cores):
                pairs.append((((x + step) % self.chips) * self.cores + c, x * self.cores + c))
        return lax.ppermute(value, "row", pairs)

    def gather(self, value):
        near = [value] + [self.shift(value, d) for d in range(1, self.chips)]
        return near + ([self.swap(p) for p in near] if self.cores > 1 else [])

    def scatter_near(self, keep, send):
        return keep + self.swap(send).astype(jnp.float32)

    def scatter_far(self, total):
        rows = total.shape[0] // self.chips
        mine = total[:rows]
        for d in range(1, self.chips):
            part = total[d * rows : (d + 1) * rows].astype(jnp.bfloat16)
            mine = mine + self.shift(part, -d).astype(jnp.float32)
        return mine.astype(jnp.bfloat16)


def shards(
    inputs,
    out_grad,
    first_vals,
    first_rows,
    first_cols,
    first_count,
    second_vals,
    second_rows,
    second_cols,
    second_count,
    *,
    hidden_blocks,
):
    n = lax.axis_size("col")
    ring = ring_of(n)
    ahead = [(ring[k], ring[(k + 1) % n]) for k in range(n)]
    back = [(b, a) for a, b in ahead]
    place = [0] * n
    for k, dev in enumerate(ring):
        place[dev] = k
    me = jnp.asarray(place, jnp.int32)[lax.axis_index("col")]

    row = Row(lax.axis_size("row"))
    x = row.gather(inputs)
    dy = row.gather(out_grad)
    width = inputs.shape[1] // BLK
    per = hidden_blocks // n
    vals = (first_vals[0, 0], second_vals[0, 0])
    slots = vals[0].shape[0]
    starts1, order1 = slot_order(first_cols[0, 0], first_rows[0, 0], first_count[0, 0], hidden_blocks)
    starts2, order2 = slot_order(second_rows[0, 0], second_cols[0, 0], second_count[0, 0], hidden_blocks)
    meta = jnp.concatenate([me[None], starts1, starts2, order1, order2])

    n_ahead = (per + 1) // 2
    parts = []
    for lo, cnt, sign in ((0, n_ahead, 1), (n_ahead, per - n_ahead, -1)):
        half = (cnt + 1) // 2
        parts.append([(lo, half, sign), (lo + half, cnt - half, sign)])
    streams = [[part[s] for part in parts if part[s][1] > 0] for s in range(2)]
    streams = [s for s in streams if s]

    def plan_of(stream, shift, parts=()):
        return Plan(stream, shift, n, per, hidden_blocks, slots, width, parts)

    def hop(stream, arrays):
        return [
            lax.ppermute(a, "col", ahead if sign > 0 else back) for a, (_, _, sign) in zip(arrays, stream)
        ]

    held = [None] * len(streams)
    x_t, grads, stores = None, [], [None] * len(streams)
    for t in range(n):
        for s, stream in enumerate(streams):
            ins = None if t == 0 else hop(stream, held[s])
            if t == 1 and s == 0:
                x_t = x.T
                ins, x_t = lax.optimization_barrier((ins, x_t))
            if t in (2, 3) and s == 0:
                grads.append(dead_call(t - 2, plan_of(stream, 0), meta, vals[t - 2]))
                ins, grads = lax.optimization_barrier((ins, grads))
            res = up_call(plan_of(stream, t + 1), meta, x, dy, vals, ins, stores[s], t == n - 1)
            if isinstance(x, list):
                x, dy = res[2:]
            held[s], stores[s] = res[:2]

    sums = None
    for t in range(n):
        for s, stream in enumerate(streams):
            if t > 0:
                held[s] = hop(stream, held[s])
                held[s], sums, grads = lax.optimization_barrier((held[s], sums, grads))
            if t < n - 1:
                res = back_call(plan_of(stream, t), meta, x_t, dy, [stores[s]], held[s], sums, grads)
                sums, grads = res[:2], res[2:]

    parts = [plan_of(stream, n - 1) for stream in streams]
    plan, acts = plan_of(sum(streams, []), n - 1, parts), sum(held, [])
    args = (plan, meta, x_t, dy, stores)
    out_near = row.scatter_near(*back_call(*args, acts, sums, None, down=(0,), with_grads=False, last=True))
    out_near, acts = lax.optimization_barrier((out_near, acts))
    in_near = row.scatter_near(*back_call(*args, acts, sums, None, down=(1,), with_grads=False, last=True))
    in_near, acts = lax.optimization_barrier((in_near, acts))
    out_sum = row.scatter_far(out_near)
    in_sum = row.scatter_far(in_near)
    grads = back_call(*args, acts, sums, grads, down=(), with_grads=True)
    return out_sum, in_sum, grads[0][None, None], grads[1][None, None]


def solution(mesh):
    hidden_blocks = 49152 // BLK // mesh.shape["row"]
    placed = (
        P("row", "col"),
        P("row", "col"),
        P("row", "col", None, None, None),
        P("row", "col", None),
        P("row", "col", None),
        P("row", "col"),
        P("row", "col", None, None, None),
        P("row", "col", None),
        P("row", "col", None),
        P("row", "col"),
    )
    return jax.shard_map(
        functools.partial(shards, hidden_blocks=hidden_blocks),
        mesh=mesh,
        in_specs=placed,
        out_specs=(
            P("row", "col"),
            P("row", "col"),
            P("row", "col", None, None, None),
            P("row", "col", None, None, None),
        ),
        check_vma=False,
    )
```

```python
import functools

import jax
import jax.numpy as jnp
from jax import lax
from jax.experimental import pallas as pl
from jax.experimental.pallas import tpu as pltpu
from jax.sharding import PartitionSpec as P

BLK = 128
Z_CHIPS = 4
ROOT_2_PI = 0.7978845608028654
CUBIC = 0.044715
VMEM_LIMIT = 40 << 20
FIRST_LIMIT = 60 << 20
FIRST_SHIFT = 20
SECOND_SHIFT = 14


def ring_of(n):
    if n % Z_CHIPS or n // Z_CHIPS < 2:
        return list(range(n))
    wide = n // Z_CHIPS
    order = [z * wide for z in range(Z_CHIPS)]
    for k, z in enumerate(reversed(range(Z_CHIPS))):
        ys = range(1, wide) if k % 2 == 0 else range(wide - 1, 0, -1)
        order += [z * wide + y for y in ys]
    return order


def gelu_pair(value, grad):
    inner = ROOT_2_PI * (value + CUBIC * (value * value * value))
    th = jnp.tanh(inner)
    half = 0.5 * (1.0 + th)
    slope = half + 0.5 * value * (1.0 - th * th) * (ROOT_2_PI * (1.0 + (3.0 * CUBIC) * (value * value)))
    return value * half, grad * slope


def slot_order(first, second, count, n_first):
    slots = first.shape[0]
    ids = jnp.arange(slots, dtype=jnp.int32)
    packed = (first << FIRST_SHIFT) | (second << SECOND_SHIFT) | ids
    key = jnp.where(ids < count, packed, jnp.iinfo(jnp.int32).max - slots + ids)
    rank = jnp.sum((key[None, :] < key[:, None]).astype(jnp.int32), axis=1)
    order = jnp.sum(jnp.where(rank[None, :] == ids[:, None], packed[None, :], 0), axis=1)
    edge = jnp.arange(n_first + 1, dtype=jnp.int32) << FIRST_SHIFT
    starts = jnp.sum((key[None, :] < edge[:, None]).astype(jnp.int32), axis=1)
    return starts, order


class Plan:
    def __init__(self, stream, shift, n, per, hidden_blocks, slots, width, parts=()):
        self.stream, self.shift, self.n, self.per = tuple(stream), shift, n, per
        self.sizes = tuple(c for _, c, _ in stream)
        self.total = sum(self.sizes)
        self.width = width
        self.parts = tuple(parts) if parts else (self,)
        self.start_at = (1, 2 + hidden_blocks)
        self.list_at = (3 + 2 * hidden_blocks, 3 + 2 * hidden_blocks + slots)

    def bases(self, meta):
        me = meta[0]
        return [lax.rem(me + (self.n - sign * self.shift) % self.n, self.n) * self.per + lo for lo, _, sign in self.stream]

    def each(self, meta, which, body):
        offset = 0
        for base, size in zip(self.bases(meta), self.sizes):
            lo = meta[self.start_at[which] + base]
            hi = meta[self.start_at[which] + base + size]

            def step(i, carry, base=base, offset=offset):
                entry = meta[self.list_at[which] + i]
                slot = entry & ((1 << SECOND_SHIFT) - 1)
                r = (entry >> SECOND_SHIFT) & ((1 << (FIRST_SHIFT - SECOND_SHIFT)) - 1)
                body(slot, (entry >> FIRST_SHIFT) - base + offset, r)
                return carry

            lax.fori_loop(lo, hi, step, 0)
            offset += size


def block_at(i):
    return pl.ds(pl.multiple_of(i * BLK, BLK), BLK)


def clear(buf):
    def step(i, carry):
        buf[block_at(i), :] = jnp.zeros((BLK, buf.shape[1]), buf.dtype)
        return carry

    lax.fori_loop(0, buf.shape[0] // BLK, step, 0)


def tile_start(plan, meta, vals, buf, sems, which):
    clear(buf)

    def go(slot, b, r):
        dst = buf.at[block_at(r), block_at(b)] if which == 0 else buf.at[block_at(b), block_at(r)]
        pltpu.make_async_copy(vals.at[slot], dst, sems.at[which, b, r]).start()

    plan.each(meta, which, go)


def tile_wait(plan, meta, vals, buf, sems, which):
    def go(slot, b, r):
        pltpu.make_async_copy(vals.at[slot], buf.at[pl.ds(0, BLK), pl.ds(0, BLK)], sems.at[which, b, r]).wait()

    plan.each(meta, which, go)


def dot_nn(a, b):
    return jnp.dot(a, b, preferred_element_type=jnp.float32)


def dot_nt(a, b):
    return lax.dot_general(a, b, (((1,), (1,)), ((), ())), preferred_element_type=jnp.float32)


def tile_loop(columns, body):
    wide = 2 * BLK if columns % (2 * BLK) == 0 else BLK
    if columns == wide:
        body(pl.ds(0, wide))
        return

    def step(i, carry):
        body(pl.ds(pl.multiple_of(i * wide, wide), wide))
        return carry

    lax.fori_loop(0, columns // wide, step, 0)


def row_loop(rows, block, body):
    def step(i, carry):
        body(pl.ds(pl.multiple_of(i * block, block), block))
        return carry

    lax.fori_loop(0, rows // block, step, 0)


def group_slices(plan):
    at, out = 0, []
    for size in plan.sizes:
        out.append(slice(at, at + size * BLK))
        at += size * BLK
    return out


class Store:
    def __init__(self, plan):
        self.side, self.rows = plan.total * BLK, plan.width * BLK
        self.cuts = plan.width // plan.total
        self.shape = (plan.n, 2 * self.rows, self.side)

    def views(self, store, step, which, buf):
        if which == 0:
            return [(store.at[step, pl.ds(0, self.rows), :], buf)]
        return [
            (store.at[step, pl.ds(self.rows + i * self.side, self.side), :], buf.at[:, pl.ds(i * self.side, self.side)])
            for i in range(self.cuts)
        ]


def keep_copies(plan, store, which, buf, sems):
    return [
        pltpu.make_async_copy(src, dst, sems.at[which, i])
        for i, (dst, src) in enumerate(Store(plan).views(store, plan.shift - 1, which, buf))
    ]


def run(copies):
    for copy in copies:
        copy.start()


def settle(copies):
    for copy in copies:
        copy.wait()


def join_copies(pieces, whole, sems):
    rows = pieces[0].shape[0]
    return [
        pltpu.make_async_copy(piece, whole.at[pl.ds(i * rows, rows), :], sems.at[i]) for i, piece in enumerate(pieces)
    ]


def up_kernel(plan, has_in, last, *refs):
    meta, x, dy, vals1, vals2 = refs[:5]
    refs = refs[5:]
    n = len(plan.sizes)
    ins = refs[:n] if has_in else None
    refs = refs[n + 1 :] if has_in else refs
    outs, refs = refs[:n], refs[n:]
    store, buf1, buf2, sems, hid, grd, keep_sems = refs
    tile_start(plan, meta, vals1, buf1, sems, 0)
    tile_start(plan, meta, vals2, buf2, sems, 1)
    tile_wait(plan, meta, vals1, buf1, sems, 0)
    keep1 = keep_copies(plan, store, 0, buf1, keep_sems)
    run(keep1)

    def hid_tile(at):
        hid[:, at] = dot_nn(x[...], buf1[:, at])

    tile_loop(plan.total * BLK, hid_tile)
    tile_wait(plan, meta, vals2, buf2, sems, 1)
    keep2 = keep_copies(plan, store, 1, buf2, keep_sems)
    run(keep2)

    def grd_tile(at):
        grd[:, at] = dot_nt(dy[...], buf2[at, :])

    tile_loop(plan.total * BLK, grd_tile)

    def join_rows(part):
        for g, at in enumerate(group_slices(plan)):
            h, d = hid[part, at], grd[part, at]
            if has_in:
                h = h + ins[g][0, part, :].astype(jnp.float32)
                d = d + ins[g][1, part, :].astype(jnp.float32)
            if last:
                h, d = gelu_pair(h, d)
            outs[g][0, part, :] = h.astype(jnp.bfloat16)
            outs[g][1, part, :] = d.astype(jnp.bfloat16)

    row_loop(hid.shape[0], BLK // 4, join_rows)
    settle(keep1 + keep2)


def first_hid_kernel(plan, n_pieces, *refs):
    meta, pieces, refs = refs[0], refs[1 : 1 + n_pieces], refs[1 + n_pieces :]
    vals1, x, hid, store, buf1, sems, keep_sems, join_sems = refs
    joins = join_copies(pieces, x, join_sems)
    run(joins)
    tile_start(plan, meta, vals1, buf1, sems, 0)
    settle(joins)
    tile_wait(plan, meta, vals1, buf1, sems, 0)
    keep = keep_copies(plan, store, 0, buf1, keep_sems)
    run(keep)

    def hid_tile(at):
        hid[:, at] = dot_nn(x[...], buf1[:, at])

    tile_loop(plan.total * BLK, hid_tile)
    settle(keep)


def first_grd_kernel(plan, n_pieces, *refs):
    meta, pieces, refs = refs[0], refs[1 : 1 + n_pieces], refs[1 + n_pieces :]
    vals2, hid, _, refs = refs[0], refs[1], refs[2], refs[3:]
    n = len(plan.sizes)
    outs, refs = refs[:n], refs[n:]
    dy, store, buf2, sems, grd, keep_sems, join_sems = refs
    joins = join_copies(pieces, dy, join_sems)
    run(joins)
    tile_start(plan, meta, vals2, buf2, sems, 1)
    settle(joins)
    tile_wait(plan, meta, vals2, buf2, sems, 1)
    keep = keep_copies(plan, store, 1, buf2, keep_sems)
    run(keep)

    def grd_tile(at):
        grd[:, at] = dot_nt(dy[...], buf2[at, :])

    tile_loop(plan.total * BLK, grd_tile)

    def join_rows(part):
        for g, at in enumerate(group_slices(plan)):
            outs[g][0, part, :] = hid[part, at].astype(jnp.bfloat16)
            outs[g][1, part, :] = grd[part, at].astype(jnp.bfloat16)

    row_loop(grd.shape[0], BLK // 4, join_rows)
    settle(keep)


def smem():
    return pl.BlockSpec(memory_space=pltpu.SMEM)


def vmem():
    return pl.BlockSpec(memory_space=pltpu.VMEM)


def hbm():
    return pl.BlockSpec(memory_space=pltpu.HBM)


def tile_scratch(total, width):
    return [
        pltpu.VMEM((width * BLK, total * BLK), jnp.bfloat16),
        pltpu.VMEM((total * BLK, width * BLK), jnp.bfloat16),
        pltpu.SemaphoreType.DMA((2, total, width)),
    ]


def up_cost(plan, tokens, products):
    side = plan.width * plan.total * BLK * BLK
    return pl.CostEstimate(
        flops=2 * products * tokens * side,
        bytes_accessed=2 * products * side + 8 * tokens * plan.total * BLK,
        transcendentals=0,
    )


def up_call(plan, meta, x, dy, vals, ins, store, last):
    tokens = x.shape[0]
    n = len(plan.sizes)
    has_in = ins is not None
    total, width = plan.total, plan.width
    shapes = [jax.ShapeDtypeStruct((2, tokens, s * BLK), jnp.bfloat16) for s in plan.sizes]
    shapes.append(jax.ShapeDtypeStruct(Store(plan).shape, jnp.bfloat16))
    res = pl.pallas_call(
        functools.partial(up_kernel, plan, has_in, last),
        out_shape=shapes,
        in_specs=[smem()] + [vmem()] * 2 + [hbm()] * 2 + ([vmem()] * n + [hbm()] if has_in else []),
        out_specs=[vmem()] * n + [hbm()],
        input_output_aliases={5 + n: n} if has_in else {},
        scratch_shapes=tile_scratch(total, width)
        + [pltpu.VMEM((tokens, total * BLK), jnp.float32)] * 2
        + [pltpu.SemaphoreType.DMA((2, Store(plan).cuts))],
        compiler_params=pltpu.CompilerParams(vmem_limit_bytes=VMEM_LIMIT),
        cost_estimate=up_cost(plan, tokens, 2),
        name="up_last" if last else "up",
    )(meta, x, dy, *vals, *((*ins, store) if has_in else ()))
    return res[:n], res[n]


def first_call(plan, meta, x, dy, vals, gather_dy):
    n_pieces = len(x)
    tokens = sum(p.shape[0] for p in x)
    n = len(plan.sizes)
    total, width = plan.total, plan.width
    buf1, buf2, sems = tile_scratch(total, width)
    whole = jax.ShapeDtypeStruct((tokens, width * BLK), jnp.bfloat16)
    store = jax.ShapeDtypeStruct(Store(plan).shape, jnp.bfloat16)
    more_sems = [
        pltpu.SemaphoreType.DMA((2, Store(plan).cuts)),
        pltpu.SemaphoreType.DMA((n_pieces,)),
    ]
    params = pltpu.CompilerParams(vmem_limit_bytes=FIRST_LIMIT)
    whole_x, hid, store = pl.pallas_call(
        functools.partial(first_hid_kernel, plan, n_pieces),
        out_shape=[whole, jax.ShapeDtypeStruct((tokens, total * BLK), jnp.float32), store],
        in_specs=[smem()] + [hbm()] * (n_pieces + 1),
        out_specs=[vmem(), vmem(), hbm()],
        scratch_shapes=[buf1, sems] + more_sems,
        compiler_params=params,
        cost_estimate=up_cost(plan, tokens, 1),
        name="first_hid",
    )(meta, *x, vals[0])
    late, hid = lax.optimization_barrier((dy[1:], hid))
    dy = gather_dy(dy[:1] + late)
    res = pl.pallas_call(
        functools.partial(first_grd_kernel, plan, n_pieces),
        out_shape=[jax.ShapeDtypeStruct((2, tokens, s * BLK), jnp.bfloat16) for s in plan.sizes]
        + [whole, jax.ShapeDtypeStruct(store.shape, store.dtype)],
        in_specs=[smem()] + [hbm()] * (n_pieces + 1) + [vmem(), hbm()],
        out_specs=[vmem()] * (n + 1) + [hbm()],
        input_output_aliases={3 + n_pieces: n + 1},
        scratch_shapes=[buf2, sems, pltpu.VMEM((tokens, total * BLK), jnp.float32)] + more_sems,
        compiler_params=params,
        cost_estimate=up_cost(plan, tokens, 1),
        name="first_grd",
    )(meta, *dy, vals[1], hid, store)
    return res[:n], res[n + 1], whole_x, res[n]


DEAD_GROUP = 16


def dead_kernel(which, plan, slots, meta, out, zeros, sems):
    zeros[...] = jnp.zeros_like(zeros)
    live = meta[plan.start_at[which] + plan.per * plan.n]
    edge = jnp.minimum((live + DEAD_GROUP - 1) // DEAD_GROUP * DEAD_GROUP, slots)

    def one(i):
        return pltpu.make_async_copy(zeros.at[0], out.at[i], sems.at[i % DEAD_GROUP])

    def many(i):
        return pltpu.make_async_copy(
            zeros, out.at[pl.ds(i * DEAD_GROUP, DEAD_GROUP)], sems.at[DEAD_GROUP + i]
        )

    def loop(lo, hi, body):
        def step(i, carry):
            body(i)
            return carry

        lax.fori_loop(lo, hi, step, 0)

    loop(edge // DEAD_GROUP, slots // DEAD_GROUP, lambda i: many(i).start())
    loop(live, edge, lambda i: one(i).start())
    loop(edge // DEAD_GROUP, slots // DEAD_GROUP, lambda i: many(i).wait())
    loop(live, edge, lambda i: one(i).wait())


def dead_call(which, plan, meta, like):
    slots = like.shape[0]
    return pl.pallas_call(
        functools.partial(dead_kernel, which, plan, slots),
        out_shape=jax.ShapeDtypeStruct(like.shape, like.dtype),
        in_specs=[smem()],
        out_specs=hbm(),
        scratch_shapes=[
            pltpu.VMEM((DEAD_GROUP, BLK, BLK), like.dtype),
            pltpu.SemaphoreType.DMA((DEAD_GROUP + slots // DEAD_GROUP,)),
        ],
        compiler_params=pltpu.CompilerParams(vmem_limit_bytes=VMEM_LIMIT),
        cost_estimate=pl.CostEstimate(flops=0, bytes_accessed=slots * BLK * BLK, transcendentals=0),
        name="dead",
    )(meta)


def back_kernel(plan, down, grads, first, last, *refs):
    meta, refs = refs[0], refs[1:]
    if grads:
        x_t, dy, refs = refs[0], refs[1], refs[2:]
    if down:
        stores, refs = refs[: len(plan.parts)], refs[len(plan.parts) :]
    n = len(plan.sizes)
    acts, refs = refs[:n], refs[n:]
    olds, outs = {}, {}
    if not first:
        for k in down:
            olds[k], refs = refs[0], refs[1:]
    if grads:
        refs = refs[2:]
    for k in down:
        outs[k], refs = (refs[:2], refs[2:]) if last else (refs[:1], refs[1:])
    if grads:
        slot_out, refs = refs[:2], refs[2:]
    act, grd = refs[:2]
    if down:
        bufs, sems = dict(zip(down, refs[2 : 2 + len(down)])), refs[2 + len(down)]
    if grads:
        act_t, stage1, stage2, out_sems = refs[-4:]
    tokens = act.shape[0]
    columns = plan.width * BLK
    loads = {}
    for k in down:
        at, loads[k] = 0, []
        for store, part in zip(stores, plan.parts):
            span = pl.ds(at * BLK, part.total * BLK)
            dst = bufs[k].at[span, :] if k == 0 else bufs[k].at[:, span]
            for src, to in Store(part).views(store, (plan.shift - 1) % plan.n, 1 - k, dst):
                loads[k].append(pltpu.make_async_copy(src, to, sems.at[k, len(loads[k])]))
            at += part.total
        for load in loads[k]:
            load.start()

    def split_rows(part):
        for a, at in zip(acts, group_slices(plan)):
            value = a[0, part, :]
            act[part, at] = value
            grd[part, at] = a[1, part, :]
            if grads:
                act_t[at, part] = value.T

    row_loop(tokens, BLK, split_rows)

    def block_of(which, b, r):
        if which == 0:
            return stage1.at[block_at(r), block_at(b)]
        return stage2.at[block_at(b), block_at(r)]

    def send(which):
        def go(slot, b, r):
            pltpu.make_async_copy(block_of(which, b, r), slot_out[which].at[slot], out_sems.at[which, b, r]).start()

        plan.each(meta, which, go)

    def drain(which):
        def go(slot, b, r):
            pltpu.make_async_copy(block_of(which, 0, 0), slot_out[which].at[slot], out_sems.at[which, b, r]).wait()

        plan.each(meta, which, go)

    def weigh(k):
        for load in loads[k]:
            load.wait()

        def tile(at):
            res = dot_nn(act[...], bufs[0][:, at]) if k == 0 else dot_nt(grd[...], bufs[1][at, :])
            if not first:
                res = res + olds[k][:, at]
            if last:
                outs[k][0][:, at] = res[: tokens // 2]
                outs[k][1][:, at] = res[tokens // 2 :].astype(jnp.bfloat16)
            else:
                outs[k][0][:, at] = res

        tile_loop(columns, tile)

    if grads:

        def first_tile(at):
            stage1[:, at] = dot_nn(x_t[...], grd[:, at]).astype(jnp.bfloat16)

        tile_loop(plan.total * BLK, first_tile)
        send(0)
    if 0 in down:
        weigh(0)
    if grads:

        def second_tile(at):
            stage2[:, at] = dot_nn(act_t[...], dy[:, at]).astype(jnp.bfloat16)

        tile_loop(columns, second_tile)
        send(1)
    if 1 in down:
        weigh(1)
    if grads:
        drain(0)
        drain(1)


def back_call(plan, meta, x_t, dy, stores, acts, sums, grads, *, down=(0, 1), with_grads=True, last=False):
    total, width = plan.total, plan.width
    tokens = acts[0].shape[1]
    n = len(plan.sizes)
    first = sums is None
    acc = jax.ShapeDtypeStruct((tokens, width * BLK), jnp.float32)
    half = [jax.ShapeDtypeStruct((tokens // 2, width * BLK), t) for t in (jnp.float32, jnp.bfloat16)]
    operands = [meta]
    specs = [smem()]
    if with_grads:
        operands += [x_t, dy]
        specs += [vmem()] * 2
    if down:
        operands += stores
        specs += [hbm()] * len(stores)
    operands += acts
    specs += [vmem()] * n
    shapes, outs, alias = [], [], {}
    for k in down:
        if not first:
            if not last:
                alias[len(operands)] = len(shapes)
            operands.append(sums[k])
            specs.append(vmem())
        shapes += half if last else [acc]
        outs += [vmem()] * (2 if last else 1)
    if with_grads:
        for k in (0, 1):
            alias[len(operands)] = len(shapes)
            operands.append(grads[k])
            specs.append(hbm())
            shapes.append(jax.ShapeDtypeStruct(grads[k].shape, jnp.bfloat16))
            outs.append(hbm())
    scratch = [pltpu.VMEM((tokens, total * BLK), jnp.bfloat16)] * 2
    if down:
        big = tile_scratch(total, width)
        scratch += [big[1 - k] for k in down] + [pltpu.SemaphoreType.DMA((2, sum(Store(p).cuts for p in plan.parts)))]
    if with_grads:
        stage1, stage2, sems = tile_scratch(total, width)
        scratch += [
            pltpu.VMEM((total * BLK, tokens), jnp.bfloat16),
            stage1,
            stage2,
            sems,
        ]
    parts = len(down) + (2 if with_grads else 0)
    return pl.pallas_call(
        functools.partial(back_kernel, plan, down, with_grads, first, last),
        out_shape=shapes,
        in_specs=specs,
        out_specs=outs,
        input_output_aliases=alias,
        scratch_shapes=scratch,
        compiler_params=pltpu.CompilerParams(vmem_limit_bytes=VMEM_LIMIT),
        cost_estimate=pl.CostEstimate(
            flops=2 * parts * tokens * width * total * BLK * BLK,
            bytes_accessed=parts * width * total * BLK * BLK,
            transcendentals=0,
        ),
        name="back",
    )(*operands)


class Row:
    def __init__(self, size):
        self.cores = 2 if size % 2 == 0 else 1
        self.chips = size // self.cores

    def swap(self, value):
        if self.cores == 1:
            return value
        return lax.ppermute(value, "row", [(k, k ^ 1) for k in range(self.chips * 2)])

    def shift(self, value, step):
        pairs = []
        for x in range(self.chips):
            for c in range(self.cores):
                pairs.append((((x + step) % self.chips) * self.cores + c, x * self.cores + c))
        return lax.ppermute(value, "row", pairs)

    def near(self, value):
        return [value] + [self.shift(value, d) for d in range(1, self.chips)]

    def far(self, near):
        return near + ([self.swap(p) for p in near] if self.cores > 1 else [])

    def scatter_near(self, keep, send):
        return keep + self.swap(send).astype(jnp.float32)

    def scatter_far(self, total):
        rows = total.shape[0] // self.chips
        mine = total[:rows]
        for d in range(1, self.chips):
            part = total[d * rows : (d + 1) * rows].astype(jnp.bfloat16)
            mine = mine + self.shift(part, -d).astype(jnp.float32)
        return mine.astype(jnp.bfloat16)


def shards(
    inputs,
    out_grad,
    first_vals,
    first_rows,
    first_cols,
    first_count,
    second_vals,
    second_rows,
    second_cols,
    second_count,
    *,
    hidden_blocks,
):
    n = lax.axis_size("col")
    ring = ring_of(n)
    ahead = [(ring[k], ring[(k + 1) % n]) for k in range(n)]
    back = [(b, a) for a, b in ahead]
    place = [0] * n
    for k, dev in enumerate(ring):
        place[dev] = k
    me = jnp.asarray(place, jnp.int32)[lax.axis_index("col")]

    row = Row(lax.axis_size("row"))
    x = row.near(inputs)
    dy = row.near(out_grad)
    width = inputs.shape[1] // BLK
    per = hidden_blocks // n
    vals = (first_vals[0, 0], second_vals[0, 0])
    slots = vals[0].shape[0]
    starts1, order1 = slot_order(first_cols[0, 0], first_rows[0, 0], first_count[0, 0], hidden_blocks)
    starts2, order2 = slot_order(second_rows[0, 0], second_cols[0, 0], second_count[0, 0], hidden_blocks)
    meta = jnp.concatenate([me[None], starts1, starts2, order1, order2])
    late, meta = lax.optimization_barrier((x[1:], meta))
    x = row.far(x[:1] + late)

    n_ahead = (per + 1) // 2
    parts = []
    for lo, cnt, sign in ((0, n_ahead, 1), (n_ahead, per - n_ahead, -1)):
        half = (cnt + 1) // 2
        parts.append([(lo, half, sign), (lo + half, cnt - half, sign)])
    streams = [[part[s] for part in parts if part[s][1] > 0] for s in range(2)]
    streams = [s for s in streams if s]

    def plan_of(stream, shift, parts=()):
        return Plan(stream, shift, n, per, hidden_blocks, slots, width, parts)

    def hop(stream, arrays):
        return [
            lax.ppermute(a, "col", ahead if sign > 0 else back) for a, (_, _, sign) in zip(arrays, stream)
        ]

    held = [None] * len(streams)
    x_t, grads, stores = None, [], [None] * len(streams)
    for t in range(n):
        for s, stream in enumerate(streams):
            ins = None if t == 0 else hop(stream, held[s])
            if t == 1 and s == 0:
                x_t = x.T
                ins, x_t = lax.optimization_barrier((ins, x_t))
            if t in (2, 3) and s == 0:
                grads.append(dead_call(t - 2, plan_of(stream, 0), meta, vals[t - 2]))
                ins, grads = lax.optimization_barrier((ins, grads))
            plan = plan_of(stream, t + 1)
            if t == 0 and s == 0:
                held[s], stores[s], x, dy = first_call(plan, meta, x, dy, vals, row.far)
            else:
                held[s], stores[s] = up_call(plan, meta, x, dy, vals, ins, stores[s], t == n - 1)

    sums = None
    for t in range(n):
        for s, stream in enumerate(streams):
            if t > 0:
                held[s] = hop(stream, held[s])
                held[s], sums, grads = lax.optimization_barrier((held[s], sums, grads))
            if t < n - 1 or s < len(streams) - 1:
                res = back_call(plan_of(stream, t), meta, x_t, dy, [stores[s]], held[s], sums, grads)
                sums, grads = res[:2], res[2:]

    acts = held[-1]
    args = (plan_of(streams[-1], n - 1), meta, x_t, dy, stores[-1:])
    out_near = row.scatter_near(*back_call(*args, acts, sums, None, down=(0,), with_grads=False, last=True))
    out_near, acts = lax.optimization_barrier((out_near, acts))
    in_near = row.scatter_near(*back_call(*args, acts, sums, None, down=(1,), with_grads=False, last=True))
    in_near, acts = lax.optimization_barrier((in_near, acts))
    out_sum = row.scatter_far(out_near)
    in_sum = row.scatter_far(in_near)
    grads = back_call(*args, acts, sums, grads, down=(), with_grads=True)
    return out_sum, in_sum, grads[0][None, None], grads[1][None, None]


def solution(mesh):
    hidden_blocks = 49152 // BLK // mesh.shape["row"]
    placed = (
        P("row", "col"),
        P("row", "col"),
        P("row", "col", None, None, None),
        P("row", "col", None),
        P("row", "col", None),
        P("row", "col"),
        P("row", "col", None, None, None),
        P("row", "col", None),
        P("row", "col", None),
        P("row", "col"),
    )
    return jax.shard_map(
        functools.partial(shards, hidden_blocks=hidden_blocks),
        mesh=mesh,
        in_specs=placed,
        out_specs=(
            P("row", "col"),
            P("row", "col"),
            P("row", "col", None, None, None),
            P("row", "col", None, None, None),
        ),
        check_vma=False,
    )
```

```python
import functools

import jax
import jax.numpy as jnp
from jax import lax
from jax.experimental import pallas as pl
from jax.experimental.pallas import tpu as pltpu
from jax.sharding import PartitionSpec as P

BLK = 128
Z_CHIPS = 4
ROOT_2_PI = 0.7978845608028654
CUBIC = 0.044715
VMEM_LIMIT = 40 << 20
FIRST_LIMIT = 44 << 20
FIRST_SHIFT = 20
SECOND_SHIFT = 14


def ring_of(n):
    if n % Z_CHIPS or n // Z_CHIPS < 2:
        return list(range(n))
    wide = n // Z_CHIPS
    order = [z * wide for z in range(Z_CHIPS)]
    for k, z in enumerate(reversed(range(Z_CHIPS))):
        ys = range(1, wide) if k % 2 == 0 else range(wide - 1, 0, -1)
        order += [z * wide + y for y in ys]
    return order


def gelu_pair(value, grad):
    inner = ROOT_2_PI * (value + CUBIC * (value * value * value))
    th = jnp.tanh(inner)
    half = 0.5 * (1.0 + th)
    slope = half + 0.5 * value * (1.0 - th * th) * (ROOT_2_PI * (1.0 + (3.0 * CUBIC) * (value * value)))
    return value * half, grad * slope


def slot_order(first, second, count, n_first):
    slots = first.shape[0]
    ids = jnp.arange(slots, dtype=jnp.int32)
    packed = (first << FIRST_SHIFT) | (second << SECOND_SHIFT) | ids
    key = jnp.where(ids < count, packed, jnp.iinfo(jnp.int32).max - slots + ids)
    rank = jnp.sum((key[None, :] < key[:, None]).astype(jnp.int32), axis=1)
    order = jnp.sum(jnp.where(rank[None, :] == ids[:, None], packed[None, :], 0), axis=1)
    edge = jnp.arange(n_first + 1, dtype=jnp.int32) << FIRST_SHIFT
    starts = jnp.sum((key[None, :] < edge[:, None]).astype(jnp.int32), axis=1)
    return starts, order


class Plan:
    def __init__(self, stream, shift, n, per, hidden_blocks, slots, width, parts=()):
        self.stream, self.shift, self.n, self.per = tuple(stream), shift, n, per
        self.sizes = tuple(c for _, c, _ in stream)
        self.total = sum(self.sizes)
        self.width = width
        self.parts = tuple(parts) if parts else (self,)
        self.start_at = (1, 2 + hidden_blocks)
        self.list_at = (3 + 2 * hidden_blocks, 3 + 2 * hidden_blocks + slots)

    def bases(self, meta):
        me = meta[0]
        return [lax.rem(me + (self.n - sign * self.shift) % self.n, self.n) * self.per + lo for lo, _, sign in self.stream]

    def each(self, meta, which, body):
        offset = 0
        for base, size in zip(self.bases(meta), self.sizes):
            lo = meta[self.start_at[which] + base]
            hi = meta[self.start_at[which] + base + size]

            def step(i, carry, base=base, offset=offset):
                entry = meta[self.list_at[which] + i]
                slot = entry & ((1 << SECOND_SHIFT) - 1)
                r = (entry >> SECOND_SHIFT) & ((1 << (FIRST_SHIFT - SECOND_SHIFT)) - 1)
                body(slot, (entry >> FIRST_SHIFT) - base + offset, r)
                return carry

            lax.fori_loop(lo, hi, step, 0)
            offset += size


def block_at(i):
    return pl.ds(pl.multiple_of(i * BLK, BLK), BLK)


def clear(buf):
    def step(i, carry):
        buf[block_at(i), :] = jnp.zeros((BLK, buf.shape[1]), buf.dtype)
        return carry

    lax.fori_loop(0, buf.shape[0] // BLK, step, 0)


def tile_start(plan, meta, vals, buf, sems, which):
    clear(buf)

    def go(slot, b, r):
        dst = buf.at[block_at(r), block_at(b)] if which == 0 else buf.at[block_at(b), block_at(r)]
        pltpu.make_async_copy(vals.at[slot], dst, sems.at[which, b, r]).start()

    plan.each(meta, which, go)


def tile_wait(plan, meta, vals, buf, sems, which):
    def go(slot, b, r):
        pltpu.make_async_copy(vals.at[slot], buf.at[pl.ds(0, BLK), pl.ds(0, BLK)], sems.at[which, b, r]).wait()

    plan.each(meta, which, go)


def dot_nn(a, b):
    return jnp.dot(a, b, preferred_element_type=jnp.float32)


def dot_nt(a, b):
    return lax.dot_general(a, b, (((1,), (1,)), ((), ())), preferred_element_type=jnp.float32)


def tile_loop(columns, body):
    wide = 2 * BLK if columns % (2 * BLK) == 0 else BLK
    if columns == wide:
        body(pl.ds(0, wide))
        return

    def step(i, carry):
        body(pl.ds(pl.multiple_of(i * wide, wide), wide))
        return carry

    lax.fori_loop(0, columns // wide, step, 0)


def row_loop(rows, block, body):
    def step(i, carry):
        body(pl.ds(pl.multiple_of(i * block, block), block))
        return carry

    lax.fori_loop(0, rows // block, step, 0)


def group_slices(plan):
    at, out = 0, []
    for size in plan.sizes:
        out.append(slice(at, at + size * BLK))
        at += size * BLK
    return out


class Store:
    def __init__(self, plan):
        self.side, self.rows = plan.total * BLK, plan.width * BLK
        self.cuts = plan.width // plan.total
        self.shape = (plan.n, 2 * self.rows, self.side)

    def views(self, store, step, which, buf):
        if which == 0:
            return [(store.at[step, pl.ds(0, self.rows), :], buf)]
        return [
            (store.at[step, pl.ds(self.rows + i * self.side, self.side), :], buf.at[:, pl.ds(i * self.side, self.side)])
            for i in range(self.cuts)
        ]


def keep_copies(plan, store, which, buf, sems):
    return [
        pltpu.make_async_copy(src, dst, sems.at[which, i])
        for i, (dst, src) in enumerate(Store(plan).views(store, plan.shift - 1, which, buf))
    ]


def run(copies):
    for copy in copies:
        copy.start()


def settle(copies):
    for copy in copies:
        copy.wait()


def join_copies(pieces, whole, sems):
    rows = pieces[0].shape[0]
    return [
        pltpu.make_async_copy(piece, whole.at[pl.ds(i * rows, rows), :], sems.at[i]) for i, piece in enumerate(pieces)
    ]


def up_kernel(plan, has_in, last, *refs):
    meta, x, dy, vals1, vals2 = refs[:5]
    refs = refs[5:]
    n = len(plan.sizes)
    ins = refs[:n] if has_in else None
    refs = refs[n + 1 :] if has_in else refs
    outs, refs = refs[:n], refs[n:]
    store, buf1, buf2, sems, hid, grd, keep_sems = refs
    tile_start(plan, meta, vals1, buf1, sems, 0)
    tile_start(plan, meta, vals2, buf2, sems, 1)
    tile_wait(plan, meta, vals1, buf1, sems, 0)
    keep1 = keep_copies(plan, store, 0, buf1, keep_sems)
    run(keep1)

    def hid_tile(at):
        hid[:, at] = dot_nn(x[...], buf1[:, at])

    tile_loop(plan.total * BLK, hid_tile)
    tile_wait(plan, meta, vals2, buf2, sems, 1)
    keep2 = keep_copies(plan, store, 1, buf2, keep_sems)
    run(keep2)

    def grd_tile(at):
        grd[:, at] = dot_nt(dy[...], buf2[at, :])

    tile_loop(plan.total * BLK, grd_tile)

    def join_rows(part):
        for g, at in enumerate(group_slices(plan)):
            h, d = hid[part, at], grd[part, at]
            if has_in:
                h = h + ins[g][0, part, :].astype(jnp.float32)
                d = d + ins[g][1, part, :].astype(jnp.float32)
            if last:
                h, d = gelu_pair(h, d)
            outs[g][0, part, :] = h.astype(jnp.bfloat16)
            outs[g][1, part, :] = d.astype(jnp.bfloat16)

    row_loop(hid.shape[0], BLK // 4, join_rows)
    settle(keep1 + keep2)


def first_hid_kernel(plan, n_pieces, *refs):
    meta, pieces, refs = refs[0], refs[1 : 1 + n_pieces], refs[1 + n_pieces :]
    vals1, x, hid, store, buf1, sems, keep_sems, join_sems = refs
    joins = join_copies(pieces, x, join_sems)
    run(joins)
    tile_start(plan, meta, vals1, buf1, sems, 0)
    settle(joins)
    tile_wait(plan, meta, vals1, buf1, sems, 0)
    keep = keep_copies(plan, store, 0, buf1, keep_sems)
    run(keep)

    def hid_tile(at):
        hid[:, at] = dot_nn(x[...], buf1[:, at])

    tile_loop(plan.total * BLK, hid_tile)
    settle(keep)


def first_grd_kernel(plan, n_pieces, *refs):
    meta, pieces, refs = refs[0], refs[1 : 1 + n_pieces], refs[1 + n_pieces :]
    vals2, hid, _, refs = refs[0], refs[1], refs[2], refs[3:]
    n = len(plan.sizes)
    outs, refs = refs[:n], refs[n:]
    dy, store, buf2, sems, grd, keep_sems, join_sems = refs
    joins = join_copies(pieces, dy, join_sems)
    run(joins)
    tile_start(plan, meta, vals2, buf2, sems, 1)
    settle(joins)
    tile_wait(plan, meta, vals2, buf2, sems, 1)
    keep = keep_copies(plan, store, 1, buf2, keep_sems)
    run(keep)

    def grd_tile(at):
        grd[:, at] = dot_nt(dy[...], buf2[at, :])

    tile_loop(plan.total * BLK, grd_tile)

    def join_rows(part):
        for g, at in enumerate(group_slices(plan)):
            outs[g][0, part, :] = hid[part, at].astype(jnp.bfloat16)
            outs[g][1, part, :] = grd[part, at].astype(jnp.bfloat16)

    row_loop(grd.shape[0], BLK // 4, join_rows)
    settle(keep)


def smem():
    return pl.BlockSpec(memory_space=pltpu.SMEM)


def vmem():
    return pl.BlockSpec(memory_space=pltpu.VMEM)


def hbm():
    return pl.BlockSpec(memory_space=pltpu.HBM)


def tile_scratch(total, width):
    return [
        pltpu.VMEM((width * BLK, total * BLK), jnp.bfloat16),
        pltpu.VMEM((total * BLK, width * BLK), jnp.bfloat16),
        pltpu.SemaphoreType.DMA((2, total, width)),
    ]


def up_cost(plan, tokens, products):
    side = plan.width * plan.total * BLK * BLK
    return pl.CostEstimate(
        flops=2 * products * tokens * side,
        bytes_accessed=2 * products * side + 8 * tokens * plan.total * BLK,
        transcendentals=0,
    )


def up_call(plan, meta, x, dy, vals, ins, store, last):
    tokens = x.shape[0]
    n = len(plan.sizes)
    has_in = ins is not None
    total, width = plan.total, plan.width
    shapes = [jax.ShapeDtypeStruct((2, tokens, s * BLK), jnp.bfloat16) for s in plan.sizes]
    shapes.append(jax.ShapeDtypeStruct(Store(plan).shape, jnp.bfloat16))
    res = pl.pallas_call(
        functools.partial(up_kernel, plan, has_in, last),
        out_shape=shapes,
        in_specs=[smem()] + [vmem()] * 2 + [hbm()] * 2 + ([vmem()] * n + [hbm()] if has_in else []),
        out_specs=[vmem()] * n + [hbm()],
        input_output_aliases={5 + n: n} if has_in else {},
        scratch_shapes=tile_scratch(total, width)
        + [pltpu.VMEM((tokens, total * BLK), jnp.float32)] * 2
        + [pltpu.SemaphoreType.DMA((2, Store(plan).cuts))],
        compiler_params=pltpu.CompilerParams(vmem_limit_bytes=VMEM_LIMIT),
        cost_estimate=up_cost(plan, tokens, 2),
        name="up_last" if last else "up",
    )(meta, x, dy, *vals, *((*ins, store) if has_in else ()))
    return res[:n], res[n]


def first_call(plan, meta, x, dy, vals, gather_dy):
    n_pieces = len(x)
    tokens = sum(p.shape[0] for p in x)
    n = len(plan.sizes)
    total, width = plan.total, plan.width
    buf1, buf2, sems = tile_scratch(total, width)
    whole = jax.ShapeDtypeStruct((tokens, width * BLK), jnp.bfloat16)
    store = jax.ShapeDtypeStruct(Store(plan).shape, jnp.bfloat16)
    more_sems = [
        pltpu.SemaphoreType.DMA((2, Store(plan).cuts)),
        pltpu.SemaphoreType.DMA((n_pieces,)),
    ]
    params = pltpu.CompilerParams(vmem_limit_bytes=FIRST_LIMIT)
    whole_x, hid, store = pl.pallas_call(
        functools.partial(first_hid_kernel, plan, n_pieces),
        out_shape=[whole, jax.ShapeDtypeStruct((tokens, total * BLK), jnp.float32), store],
        in_specs=[smem()] + [hbm()] * (n_pieces + 1),
        out_specs=[vmem(), vmem(), hbm()],
        scratch_shapes=[buf1, sems] + more_sems,
        compiler_params=params,
        cost_estimate=up_cost(plan, tokens, 1),
        name="first_hid",
    )(meta, *x, vals[0])
    late, hid = lax.optimization_barrier((dy[1:], hid))
    dy = gather_dy(dy[:1] + late)
    res = pl.pallas_call(
        functools.partial(first_grd_kernel, plan, n_pieces),
        out_shape=[jax.ShapeDtypeStruct((2, tokens, s * BLK), jnp.bfloat16) for s in plan.sizes]
        + [whole, jax.ShapeDtypeStruct(store.shape, store.dtype)],
        in_specs=[smem()] + [hbm()] * (n_pieces + 1) + [vmem(), hbm()],
        out_specs=[vmem()] * (n + 1) + [hbm()],
        input_output_aliases={3 + n_pieces: n + 1},
        scratch_shapes=[buf2, sems, pltpu.VMEM((tokens, total * BLK), jnp.float32)] + more_sems,
        compiler_params=params,
        cost_estimate=up_cost(plan, tokens, 1),
        name="first_grd",
    )(meta, *dy, vals[1], hid, store)
    return res[:n], res[n + 1], whole_x, res[n]


DEAD_GROUP = 16


def dead_kernel(which, plan, slots, meta, out, zeros, sems):
    zeros[...] = jnp.zeros_like(zeros)
    live = meta[plan.start_at[which] + plan.per * plan.n]
    edge = jnp.minimum((live + DEAD_GROUP - 1) // DEAD_GROUP * DEAD_GROUP, slots)

    def one(i):
        return pltpu.make_async_copy(zeros.at[0], out.at[i], sems.at[i % DEAD_GROUP])

    def many(i):
        return pltpu.make_async_copy(
            zeros, out.at[pl.ds(i * DEAD_GROUP, DEAD_GROUP)], sems.at[DEAD_GROUP + i]
        )

    def loop(lo, hi, body):
        def step(i, carry):
            body(i)
            return carry

        lax.fori_loop(lo, hi, step, 0)

    loop(edge // DEAD_GROUP, slots // DEAD_GROUP, lambda i: many(i).start())
    loop(live, edge, lambda i: one(i).start())
    loop(edge // DEAD_GROUP, slots // DEAD_GROUP, lambda i: many(i).wait())
    loop(live, edge, lambda i: one(i).wait())


def dead_call(which, plan, meta, like):
    slots = like.shape[0]
    return pl.pallas_call(
        functools.partial(dead_kernel, which, plan, slots),
        out_shape=jax.ShapeDtypeStruct(like.shape, like.dtype),
        in_specs=[smem()],
        out_specs=hbm(),
        scratch_shapes=[
            pltpu.VMEM((DEAD_GROUP, BLK, BLK), like.dtype),
            pltpu.SemaphoreType.DMA((DEAD_GROUP + slots // DEAD_GROUP,)),
        ],
        compiler_params=pltpu.CompilerParams(vmem_limit_bytes=VMEM_LIMIT),
        cost_estimate=pl.CostEstimate(flops=0, bytes_accessed=slots * BLK * BLK, transcendentals=0),
        name="dead",
    )(meta)


def back_kernel(plan, down, grads, first, last, *refs):
    meta, refs = refs[0], refs[1:]
    if grads:
        x_t, dy, refs = refs[0], refs[1], refs[2:]
    if down:
        stores, refs = refs[: len(plan.parts)], refs[len(plan.parts) :]
    n = len(plan.sizes)
    acts, refs = refs[:n], refs[n:]
    olds, outs = {}, {}
    if not first:
        for k in down:
            olds[k], refs = refs[0], refs[1:]
    if grads:
        refs = refs[2:]
    for k in down:
        outs[k], refs = (refs[:2], refs[2:]) if last else (refs[:1], refs[1:])
    if grads:
        slot_out, refs = refs[:2], refs[2:]
    act, grd = refs[:2]
    if down:
        bufs, sems = dict(zip(down, refs[2 : 2 + len(down)])), refs[2 + len(down)]
    if grads:
        act_t, stage1, stage2, out_sems = refs[-4:]
    tokens = act.shape[0]
    columns = plan.width * BLK
    loads = {}
    for k in down:
        at, loads[k] = 0, []
        for store, part in zip(stores, plan.parts):
            span = pl.ds(at * BLK, part.total * BLK)
            dst = bufs[k].at[span, :] if k == 0 else bufs[k].at[:, span]
            for src, to in Store(part).views(store, (plan.shift - 1) % plan.n, 1 - k, dst):
                loads[k].append(pltpu.make_async_copy(src, to, sems.at[k, len(loads[k])]))
            at += part.total
        for load in loads[k]:
            load.start()

    def split_rows(part):
        for a, at in zip(acts, group_slices(plan)):
            value = a[0, part, :]
            act[part, at] = value
            grd[part, at] = a[1, part, :]
            if grads:
                act_t[at, part] = value.T

    row_loop(tokens, BLK, split_rows)

    def block_of(which, b, r):
        if which == 0:
            return stage1.at[block_at(r), block_at(b)]
        return stage2.at[block_at(b), block_at(r)]

    def send(which):
        def go(slot, b, r):
            pltpu.make_async_copy(block_of(which, b, r), slot_out[which].at[slot], out_sems.at[which, b, r]).start()

        plan.each(meta, which, go)

    def drain(which):
        def go(slot, b, r):
            pltpu.make_async_copy(block_of(which, 0, 0), slot_out[which].at[slot], out_sems.at[which, b, r]).wait()

        plan.each(meta, which, go)

    def weigh(k):
        for load in loads[k]:
            load.wait()

        def tile(at):
            res = dot_nn(act[...], bufs[0][:, at]) if k == 0 else dot_nt(grd[...], bufs[1][at, :])
            if not first:
                res = res + olds[k][:, at]
            if last:
                outs[k][0][:, at] = res[: tokens // 2]
                outs[k][1][:, at] = res[tokens // 2 :].astype(jnp.bfloat16)
            else:
                outs[k][0][:, at] = res

        tile_loop(columns, tile)

    if grads:

        def first_tile(at):
            stage1[:, at] = dot_nn(x_t[...], grd[:, at]).astype(jnp.bfloat16)

        tile_loop(plan.total * BLK, first_tile)
        send(0)
    if 0 in down:
        weigh(0)
    if grads:

        def second_tile(at):
            stage2[:, at] = dot_nn(act_t[...], dy[:, at]).astype(jnp.bfloat16)

        tile_loop(columns, second_tile)
        send(1)
    if 1 in down:
        weigh(1)
    if grads:
        drain(0)
        drain(1)


def back_call(plan, meta, x_t, dy, stores, acts, sums, grads, *, down=(0, 1), with_grads=True, last=False):
    total, width = plan.total, plan.width
    tokens = acts[0].shape[1]
    n = len(plan.sizes)
    first = sums is None
    acc = jax.ShapeDtypeStruct((tokens, width * BLK), jnp.float32)
    half = [jax.ShapeDtypeStruct((tokens // 2, width * BLK), t) for t in (jnp.float32, jnp.bfloat16)]
    operands = [meta]
    specs = [smem()]
    if with_grads:
        operands += [x_t, dy]
        specs += [vmem()] * 2
    if down:
        operands += stores
        specs += [hbm()] * len(stores)
    operands += acts
    specs += [vmem()] * n
    shapes, outs, alias = [], [], {}
    for k in down:
        if not first:
            if not last:
                alias[len(operands)] = len(shapes)
            operands.append(sums[k])
            specs.append(vmem())
        shapes += half if last else [acc]
        outs += [vmem()] * (2 if last else 1)
    if with_grads:
        for k in (0, 1):
            alias[len(operands)] = len(shapes)
            operands.append(grads[k])
            specs.append(hbm())
            shapes.append(jax.ShapeDtypeStruct(grads[k].shape, jnp.bfloat16))
            outs.append(hbm())
    scratch = [pltpu.VMEM((tokens, total * BLK), jnp.bfloat16)] * 2
    if down:
        big = tile_scratch(total, width)
        scratch += [big[1 - k] for k in down] + [pltpu.SemaphoreType.DMA((2, sum(Store(p).cuts for p in plan.parts)))]
    if with_grads:
        stage1, stage2, sems = tile_scratch(total, width)
        scratch += [
            pltpu.VMEM((total * BLK, tokens), jnp.bfloat16),
            stage1,
            stage2,
            sems,
        ]
    parts = len(down) + (2 if with_grads else 0)
    return pl.pallas_call(
        functools.partial(back_kernel, plan, down, with_grads, first, last),
        out_shape=shapes,
        in_specs=specs,
        out_specs=outs,
        input_output_aliases=alias,
        scratch_shapes=scratch,
        compiler_params=pltpu.CompilerParams(vmem_limit_bytes=VMEM_LIMIT),
        cost_estimate=pl.CostEstimate(
            flops=2 * parts * tokens * width * total * BLK * BLK,
            bytes_accessed=parts * width * total * BLK * BLK,
            transcendentals=0,
        ),
        name="back",
    )(*operands)


class Row:
    def __init__(self, size):
        self.cores = 2 if size % 2 == 0 else 1
        self.chips = size // self.cores

    def swap(self, value):
        if self.cores == 1:
            return value
        return lax.ppermute(value, "row", [(k, k ^ 1) for k in range(self.chips * 2)])

    def shift(self, value, step):
        pairs = []
        for x in range(self.chips):
            for c in range(self.cores):
                pairs.append((((x + step) % self.chips) * self.cores + c, x * self.cores + c))
        return lax.ppermute(value, "row", pairs)

    def near(self, value):
        return [value] + [self.shift(value, d) for d in range(1, self.chips)]

    def far(self, near):
        return near + ([self.swap(p) for p in near] if self.cores > 1 else [])

    def scatter_near(self, keep, send):
        return keep + self.swap(send).astype(jnp.float32)

    def scatter_far(self, total):
        rows = total.shape[0] // self.chips
        mine = total[:rows]
        for d in range(1, self.chips):
            part = total[d * rows : (d + 1) * rows].astype(jnp.bfloat16)
            mine = mine + self.shift(part, -d).astype(jnp.float32)
        return mine.astype(jnp.bfloat16)


def shards(
    inputs,
    out_grad,
    first_vals,
    first_rows,
    first_cols,
    first_count,
    second_vals,
    second_rows,
    second_cols,
    second_count,
    *,
    hidden_blocks,
):
    n = lax.axis_size("col")
    ring = ring_of(n)
    ahead = [(ring[k], ring[(k + 1) % n]) for k in range(n)]
    back = [(b, a) for a, b in ahead]
    place = [0] * n
    for k, dev in enumerate(ring):
        place[dev] = k
    me = jnp.asarray(place, jnp.int32)[lax.axis_index("col")]

    row = Row(lax.axis_size("row"))
    x = row.near(inputs)
    dy = row.near(out_grad)
    width = inputs.shape[1] // BLK
    per = hidden_blocks // n
    vals = (first_vals[0, 0], second_vals[0, 0])
    slots = vals[0].shape[0]
    starts1, order1 = slot_order(first_cols[0, 0], first_rows[0, 0], first_count[0, 0], hidden_blocks)
    starts2, order2 = slot_order(second_rows[0, 0], second_cols[0, 0], second_count[0, 0], hidden_blocks)
    meta = jnp.concatenate([me[None], starts1, starts2, order1, order2])
    late, meta = lax.optimization_barrier((x[1:], meta))
    x = row.far(x[:1] + late)

    n_ahead = (per + 1) // 2
    parts = []
    for lo, cnt, sign in ((0, n_ahead, 1), (n_ahead, per - n_ahead, -1)):
        half = (cnt + 1) // 2
        parts.append([(lo, half, sign), (lo + half, cnt - half, sign)])
    streams = [[part[s] for part in parts if part[s][1] > 0] for s in range(2)]
    streams = [s for s in streams if s]

    def plan_of(stream, shift, parts=()):
        return Plan(stream, shift, n, per, hidden_blocks, slots, width, parts)

    def hop(stream, arrays):
        return [
            lax.ppermute(a, "col", ahead if sign > 0 else back) for a, (_, _, sign) in zip(arrays, stream)
        ]

    held = [None] * len(streams)
    x_t, grads, stores = None, [], [None] * len(streams)
    for t in range(n):
        for s, stream in enumerate(streams):
            ins = None if t == 0 else hop(stream, held[s])
            if t == 1 and s == 0:
                x_t = x.T
                ins, x_t = lax.optimization_barrier((ins, x_t))
            if t in (2, 3) and s == 0:
                grads.append(dead_call(t - 2, plan_of(stream, 0), meta, vals[t - 2]))
                ins, grads = lax.optimization_barrier((ins, grads))
            plan = plan_of(stream, t + 1)
            if t == 0 and s == 0:
                held[s], stores[s], x, dy = first_call(plan, meta, x, dy, vals, row.far)
            else:
                held[s], stores[s] = up_call(plan, meta, x, dy, vals, ins, stores[s], t == n - 1)

    sums = None
    for t in range(n):
        for s, stream in enumerate(streams):
            if t > 0:
                held[s] = hop(stream, held[s])
                held[s], sums, grads = lax.optimization_barrier((held[s], sums, grads))
            if t < n - 1 or s < len(streams) - 1:
                res = back_call(plan_of(stream, t), meta, x_t, dy, [stores[s]], held[s], sums, grads)
                sums, grads = res[:2], res[2:]

    acts = held[-1]
    args = (plan_of(streams[-1], n - 1), meta, x_t, dy, stores[-1:])
    out_near = row.scatter_near(*back_call(*args, acts, sums, None, down=(0,), with_grads=False, last=True))
    out_near, acts = lax.optimization_barrier((out_near, acts))
    in_near = row.scatter_near(*back_call(*args, acts, sums, None, down=(1,), with_grads=False, last=True))
    in_near, acts = lax.optimization_barrier((in_near, acts))
    out_sum = row.scatter_far(out_near)
    in_sum = row.scatter_far(in_near)
    grads = back_call(*args, acts, sums, grads, down=(), with_grads=True)
    return out_sum, in_sum, grads[0][None, None], grads[1][None, None]


def solution(mesh):
    hidden_blocks = 49152 // BLK // mesh.shape["row"]
    placed = (
        P("row", "col"),
        P("row", "col"),
        P("row", "col", None, None, None),
        P("row", "col", None),
        P("row", "col", None),
        P("row", "col"),
        P("row", "col", None, None, None),
        P("row", "col", None),
        P("row", "col", None),
        P("row", "col"),
    )
    return jax.shard_map(
        functools.partial(shards, hidden_blocks=hidden_blocks),
        mesh=mesh,
        in_specs=placed,
        out_specs=(
            P("row", "col"),
            P("row", "col"),
            P("row", "col", None, None, None),
            P("row", "col", None, None, None),
        ),
        check_vma=False,
    )
```
